32 devices in a mesh: row: 4 (over y, x), col: 8 (over z, core).
Axes of the slice: x: 2, y: 2, z: 4, core: 2. Of those that a mesh axis runs over, the one named last changes fastest.
Arguments:
- scalar_field: float32 [256, 256, 1024], P('col', 'row'), may hold values from -1.2 to 1.2
- reaction: float32 [256, 256, 1024], P('col', 'row'), may hold values from 0.5 to 4
- x_faces: float32 [1024], replicated, may hold values from 0.5 to 4
- y_faces: float32 [256], replicated, may hold values from 0.5 to 4
- z_faces: float32 [256], replicated, may hold values from 0.5 to 4
- x_inverse: float32 [8, 128, 128], replicated, may hold values from 0 to 1, as said below
- y_inverse: float32 [2, 128, 128], replicated, may hold values from 0 to 1, as said below
- z_inverse: float32 [2, 128, 128], replicated, may hold values from 0 to 1, as said below
Outputs:
- advanced: float32 [256, 256, 1024], P('col', 'row')
The draws below stay inside these ranges and needn't reach their ends.
Inputs may be any that keep to these rules, and one draw needn't show every extreme that they name: x_inverse[c] is, up to float32 rounding, the inverse of the block of rows and columns c * 128 to (c + 1) * 128 - 1 of the matrix I - 500 A_x along one x line. y_inverse[c] is, up to float32 rounding, the inverse of the block of rows and columns c * 128 to (c + 1) * 128 - 1 of the matrix I - 500 A_y along one y line. z_inverse[c] is, up to float32 rounding, the inverse of the block of rows and columns c * 128 to (c + 1) * 128 - 1 of the matrix I - 500 A_z along one z line.
All inputs are finite; a program needn't handle non-finite values.
Results may differ from the reference program's by a relative error of at most 0.0003.
Values sent between devices are 32-bit elements; how exact they have to be, the bound alone decides.
A program may use at most 128 MiB of HBM per device.

```python
import math
import jax
import jax.numpy as jnp
from jax import lax

NY = 256
NZ = 256
GROUP = 128
NX = 1024


implicit_weight = 0.5


time_step = 1000.0


def invert_small_drawn(matrix):
    order = matrix.shape[0]
    joined = jnp.concatenate([matrix, jnp.eye(order, dtype=matrix.dtype)], axis=1)

    def sweep(step_index, current):
        pivot_row = lax.dynamic_index_in_dim(current, step_index, 0, keepdims=False)
        pivot_row = pivot_row / lax.dynamic_index_in_dim(pivot_row, step_index, 0, keepdims=False)
        pivot_column = lax.dynamic_slice_in_dim(current, step_index, 1, 1)
        current = current - pivot_column * pivot_row[None, :]
        return lax.dynamic_update_index_in_dim(current, pivot_row, step_index, 0)
    joined = lax.fori_loop(0, order, sweep, joined)
    return joined[:, order:]


def faces_and_blocks(key, length):
    face_values = jnp.exp(jax.random.uniform(key, (length,), jnp.float32, math.log(0.5), math.log(4.0)))
    couple = implicit_weight * time_step * face_values
    couple_above = jnp.concatenate([couple[1:], jnp.zeros((1,), jnp.float32)])
    groups = length // GROUP
    diagonal = (1.0 + couple + couple_above).reshape(groups, GROUP)
    upper_band = couple_above.reshape(groups, GROUP)[:, :, None] * jnp.eye(GROUP, k=1, dtype=jnp.float32)
    blocks = diagonal[:, :, None] * jnp.eye(GROUP, dtype=jnp.float32) - upper_band - jnp.swapaxes(upper_band, 1, 2)
    return (face_values, jax.vmap(invert_small_drawn)(blocks))


def draw_x_faces(key, part):
    return faces_and_blocks(jax.random.fold_in(key, 101), NX)[0]


def draw_x_inverse(key, part):
    return faces_and_blocks(jax.random.fold_in(key, 101), NX)[1]


def draw_y_faces(key, part):
    return faces_and_blocks(jax.random.fold_in(key, 202), NY)[0]


def draw_y_inverse(key, part):
    return faces_and_blocks(jax.random.fold_in(key, 202), NY)[1]


def draw_z_faces(key, part):
    return faces_and_blocks(jax.random.fold_in(key, 303), NZ)[0]


def draw_z_inverse(key, part):
    return faces_and_blocks(jax.random.fold_in(key, 303), NZ)[1]


def levels(stream_key, dims, cuts, least, high):
    def one(position, parts):
        heights = jax.random.uniform(jax.random.fold_in(jax.random.fold_in(stream_key, 6), position), (parts,), jnp.float32, least / len(cuts), high / len(cuts))
        return jnp.repeat(jnp.exp(heights), dims[position] // parts).reshape((-1,) + (1,) * (len(dims) - position - 1))

    level = one(*cuts[0])
    for cut in cuts[1:]:
        level = level * one(*cut)
    return level


def setup_inputs(seed: int = 0) -> dict:
    seeds = jax.random.split(jax.random.key(seed), 9)
    return {
        "scalar_field": jnp.clip(jax.random.uniform(seeds[0], (NZ, NY, NX), jnp.float32, -1.2, 1.2) * levels(seeds[0], (NZ, NY, NX), ((0, 8), (1, 4)), -0.4, 0.0), -1.2, 1.2),
        "reaction": jnp.clip(jnp.exp(math.log(4.0) - 2.0794415 * jax.random.uniform(seeds[1], (NZ, NY, NX), jnp.float32) ** levels(seeds[1], (NZ, NY, NX), ((0, 8), (1, 4)), -0.2, 0.2)), 0.5, 4.0),
        "x_faces": draw_x_faces(jax.random.fold_in(seeds[8], 71), 0),
        "y_faces": draw_y_faces(jax.random.fold_in(seeds[8], 71), 0),
        "z_faces": draw_z_faces(jax.random.fold_in(seeds[8], 71), 0),
        "x_inverse": draw_x_inverse(jax.random.fold_in(seeds[8], 71), 0),
        "y_inverse": draw_y_inverse(jax.random.fold_in(seeds[8], 71), 0),
        "z_inverse": draw_z_inverse(jax.random.fold_in(seeds[8], 71), 0),
    }


implicit_weight = 0.5
time_step = 1000.0


def shift_lower(values, line_axis):
    length = values.shape[line_axis]
    first_slot = jnp.zeros_like(lax.slice_in_dim(values, 0, 1, axis=line_axis))
    return jnp.concatenate([first_slot, lax.slice_in_dim(values, 0, length - 1, axis=line_axis)], axis=line_axis)


def shift_upper(values, line_axis):
    length = values.shape[line_axis]
    last_slot = jnp.zeros_like(lax.slice_in_dim(values, 0, 1, axis=line_axis))
    return jnp.concatenate([lax.slice_in_dim(values, 1, length, axis=line_axis), last_slot], axis=line_axis)


def apply_line(values, face_values, line_axis):
    spread = [1, 1, 1]
    spread[line_axis] = values.shape[line_axis]
    face_here = face_values.reshape(spread)
    face_next = jnp.concatenate([face_values[1:], jnp.zeros((1,), face_values.dtype)]).reshape(spread)
    lower_value = shift_lower(values, line_axis)
    upper_value = shift_upper(values, line_axis)
    return face_next * (upper_value - values) - face_here * (values - lower_value)


def invert_small(matrix):
    order = matrix.shape[0]
    joined = jnp.concatenate([matrix, jnp.eye(order, dtype=matrix.dtype)], axis=1)

    def sweep(step_index, current):
        pivot_row = lax.dynamic_index_in_dim(current, step_index, 0, keepdims=False)
        pivot_row = pivot_row / lax.dynamic_index_in_dim(pivot_row, step_index, 0, keepdims=False)
        pivot_column = lax.dynamic_slice_in_dim(current, step_index, 1, 1)
        current = current - pivot_column * pivot_row[None, :]
        return lax.dynamic_update_index_in_dim(current, pivot_row, step_index, 0)

    joined = lax.fori_loop(0, order, sweep, joined)
    return joined[:, order:]


def reduced_inverse(inverse, coupling_before, coupling_after):
    groups, block_width = inverse.shape[0], inverse.shape[1]
    order = 2 * groups
    group_index = jnp.arange(groups)
    lead_rows = 2 * group_index
    trail_rows = 2 * group_index + 1
    prev_cols = jnp.maximum(2 * group_index - 1, 0)
    next_cols = jnp.minimum(2 * group_index + 2, order - 1)
    coupled = jnp.zeros((order, order), inverse.dtype)
    coupled = coupled.at[lead_rows, prev_cols].add(coupling_before * inverse[:, 0, 0])
    coupled = coupled.at[lead_rows, next_cols].add(coupling_after * inverse[:, 0, block_width - 1])
    coupled = coupled.at[trail_rows, prev_cols].add(coupling_before * inverse[:, block_width - 1, 0])
    coupled = coupled.at[trail_rows, next_cols].add(coupling_after * inverse[:, block_width - 1, block_width - 1])
    return invert_small(jnp.eye(order, dtype=inverse.dtype) - coupled)


def line_solve(right_side, inverse, face_values, line_axis):
    groups, block_width = inverse.shape[0], inverse.shape[1]
    dims_full = right_side.shape
    blocked = right_side.reshape(dims_full[:line_axis] + (groups, block_width) + dims_full[line_axis + 1:])
    others = ["u", "v"]
    source = "".join(others[:line_axis] + ["c", "j"] + others[line_axis:])
    target = "".join(others[:line_axis] + ["c", "i"] + others[line_axis:])
    inside = jnp.einsum("cij," + source + "->" + target, inverse, blocked, precision=lax.Precision.HIGHEST)
    leading = lax.index_in_dim(inside, 0, line_axis + 1, keepdims=False)
    trailing = lax.index_in_dim(inside, block_width - 1, line_axis + 1, keepdims=False)
    coupling = implicit_weight * time_step * face_values[block_width::block_width]
    nothing = jnp.zeros((1,), face_values.dtype)
    coupling_before = jnp.concatenate([nothing, coupling])
    coupling_after = jnp.concatenate([coupling, nothing])
    reduced = reduced_inverse(inverse, coupling_before, coupling_after)
    interface = jnp.stack([leading, trailing], axis=line_axis + 1)
    interface = interface.reshape(dims_full[:line_axis] + (2 * groups,) + dims_full[line_axis + 1:])
    end_source = "".join(others[:line_axis] + ["j"] + others[line_axis:])
    end_target = "".join(others[:line_axis] + ["i"] + others[line_axis:])
    solved = jnp.einsum("ij," + end_source + "->" + end_target, reduced, interface, precision=lax.Precision.HIGHEST)
    solved = solved.reshape(dims_full[:line_axis] + (groups, 2) + dims_full[line_axis + 1:])
    first_values = lax.index_in_dim(solved, 0, line_axis + 1, keepdims=False)
    last_values = lax.index_in_dim(solved, 1, line_axis + 1, keepdims=False)
    prev_last = shift_lower(last_values, line_axis)
    next_first = shift_upper(first_values, line_axis)
    spike_shape = [1, 1, 1, 1]
    spike_shape[line_axis] = groups
    spike_shape[line_axis + 1] = block_width
    left_spike = (coupling_before[:, None] * inverse[:, :, 0]).reshape(spike_shape)
    right_spike = (coupling_after[:, None] * inverse[:, :, block_width - 1]).reshape(spike_shape)
    result = inside + left_spike * jnp.expand_dims(prev_last, line_axis + 1) + right_spike * jnp.expand_dims(next_first, line_axis + 1)
    return result.reshape(dims_full)


def reference(scalar_field, reaction, x_faces, y_faces, z_faces, x_inverse, y_inverse, z_inverse):
    x_term = apply_line(scalar_field, x_faces, 2)
    y_term = apply_line(scalar_field, y_faces, 1)
    z_term = apply_line(scalar_field, z_faces, 0)
    source = reaction * scalar_field * (1.0 - scalar_field * scalar_field)
    explicit = scalar_field + time_step * (x_term + y_term + z_term + source) - implicit_weight * time_step * x_term
    first_section = line_solve(explicit, x_inverse, x_faces, 2)
    second_section = line_solve(first_section - implicit_weight * time_step * y_term, y_inverse, y_faces, 1)
    return line_solve(second_section - implicit_weight * time_step * z_term, z_inverse, z_faces, 0)
```

```python
import functools

import jax
import jax.numpy as jnp
from jax import lax
from jax.experimental import pallas as pl
from jax.experimental.pallas import tpu as pltpu
from jax.sharding import PartitionSpec as P

WEIGHT = 0.5
STEP = 1000.0
MESH = pl.DeviceIdType.MESH
LANES = 128
MAIN_VMEM = 24 * 1024 * 1024
LAST_VMEM = 12 * 1024 * 1024


def shifted(a, by, fill):
    n = a.shape[1]
    lane = lax.broadcasted_iota(jnp.int32, a.shape, 1)
    if by > 0:
        return jnp.where(lane >= by, pltpu.roll(a, by, 1), fill)
    return jnp.where(lane < n + by, pltpu.roll(a, n + by, 1), fill)


def running_sum(a):
    by = 1
    while by < a.shape[1]:
        a = a + shifted(a, by, 0.0)
        by *= 2
    return a


def ladder(couple, sign):
    p00, p01, p10, p11 = 1.0 + couple, couple, jnp.ones_like(couple), couple
    by = 1
    while by < couple.shape[1]:
        q00, q01 = shifted(p00, sign * by, 1.0), shifted(p01, sign * by, 0.0)
        q10, q11 = shifted(p10, sign * by, 0.0), shifted(p11, sign * by, 1.0)
        n00, n01 = p00 * q00 + p01 * q10, p00 * q01 + p01 * q11
        n10, n11 = p10 * q00 + p11 * q10, p10 * q01 + p11 * q11
        scale = 1.0 / (n00 + n01 + n10 + n11)
        p00, p01, p10, p11 = n00 * scale, n01 * scale, n10 * scale, n11 * scale
        by *= 2
    return p00 / p10


def as_column(line, rows):
    n = line.shape[1]
    return jnp.transpose(jnp.broadcast_to(line, (n, n)))[:rows, :rows]


def block_of_inverse(diagonal, sums, n):
    i = lax.broadcasted_iota(jnp.int32, (n, n), 0)
    j = lax.broadcasted_iota(jnp.int32, (n, n), 1)
    near = jnp.where(i >= j, diagonal[:, :n], as_column(diagonal, n))
    return near * jnp.exp(-jnp.abs(as_column(sums, n) - sums[:, :n]))


def split(a):
    high = a.astype(jnp.bfloat16)
    return high, (a - high.astype(jnp.float32)).astype(jnp.bfloat16)


def dot(a, b):
    return jnp.dot(a, b, preferred_element_type=jnp.float32)


def lanes_of(column):
    return jnp.broadcast_to(column, (column.shape[0], LANES))


def x_solve(rows_of, xw, xpass, xthrough, nt):
    nb, bx = xw.shape[0], xw.shape[2]
    per = bx // LANES
    local = []
    for b in range(nb):
        high, low = split(jnp.concatenate([rows_of(b * per + i) for i in range(per)], axis=1))
        local.append(dot(jnp.concatenate([high, low, high], axis=1), xw[b]))
    left, right = [None], [None]
    for b in range(nb - 1):
        value = lanes_of(local[b][:, bx - 1:bx])
        if b:
            value = value + left[-1] * xthrough[0, b:b + 1]
        left.append(value)
        c = nb - 1 - b
        value = lanes_of(local[c][:, 0:1])
        if b:
            value = value + right[-1] * xthrough[1, c:c + 1]
        right.append(value)
    right.reverse()
    solved = []
    for t in range(nt):
        b, i = t // per, t % per
        value = local[b][:, i * LANES:(i + 1) * LANES]
        if b:
            value = value + xpass[0, t:t + 1] * left[b]
        if b < nb - 1:
            value = value + xpass[1, t:t + 1] * right[b]
        solved.append(value)
    return solved


def main_kernel(
    nr, nc, planes, xf_hbm, yf_hbm, zf_hbm, field_ref, rea_ref,
    base, sy_ref, sz_ref, zpass, ypass,
    faces, u, edges, yhalo, coef, xface, yface, ztab, xline, xw, xpass, xthrough, ym, weights,
    vprev, zedge, zsend, zbuf, ye, ybuf, esend, ebuf, fill,
    face_sem, u_sem, rea_sem, hsend, hrecv, zsend_sem, zrecv_sem,
    ysend_sem, yrecv_sem, esend_sem, erecv_sem,
):
    row, col = lax.axis_index("row"), lax.axis_index("col")
    nt, zc, yc, _ = base.shape
    nx = nt * LANES
    nk = yc // 8
    length = faces.shape[2]
    f32 = jnp.float32

    face_copies = [
        pltpu.make_async_copy(
            a, faces.at[i, pl.ds(0, 1), pl.ds(0, a.shape[1])], face_sem.at[i]
        )
        for i, a in enumerate((xf_hbm, yf_hbm, zf_hbm))
    ]
    for i, a in enumerate((xf_hbm, yf_hbm, zf_hbm)):
        if a.shape[1] < length:
            faces[i, 0:1, a.shape[1]:] = jnp.zeros((1, length - a.shape[1]), f32)
    for copy in face_copies:
        copy.start()
    u_copies = [
        pltpu.make_async_copy(
            field_ref.at[:, :, pl.ds(t * LANES, LANES)], u.at[t, :, pl.ds(8, yc)], u_sem.at[t]
        )
        for t in range(nt)
    ]
    for copy in u_copies:
        copy.start()

    up_row, down_row = row < nr - 1, row > 0
    has_low, has_high = col > 0, col < nc - 1
    barrier = pltpu.get_barrier_semaphore()
    for other in range(nr):
        @pl.when(other != row)
        def _():
            pl.semaphore_signal(barrier, inc=1, device_id=(other, col), device_id_type=MESH)

    @pl.when(has_low)
    def _():
        pl.semaphore_signal(barrier, inc=1, device_id=(row, col - 1), device_id_type=MESH)

    @pl.when(has_high)
    def _():
        pl.semaphore_signal(barrier, inc=1, device_id=(row, col + 1), device_id_type=MESH)

    vprev[...] = jnp.zeros_like(vprev)
    for side, source, there in ((0, has_low, down_row), (1, has_high, up_row)):
        @pl.when(jnp.logical_not(source))
        def _():
            zbuf[side] = jnp.zeros(zbuf.shape[1:], f32)

        @pl.when(jnp.logical_not(there))
        def _():
            yhalo[side] = jnp.zeros(yhalo.shape[1:], f32)

    for copy in face_copies:
        copy.wait()

    lines = jnp.concatenate([faces[0, 0:1], faces[1, 0:1], faces[2, 0:1], jnp.zeros((5, length), f32)], axis=0)
    here = WEIGHT * STEP * lines
    above = shifted(here, -1, 0.0)
    e = ladder(here, 1)
    h = ladder(above, -1)
    pivot = above + e
    down = above / pivot
    inverse = 1.0 / pivot
    diag = 1.0 / (e + h - 1.0)
    ups = running_sum(jnp.log(jnp.maximum(here / (here + h), 1e-30)))
    downs = running_sum(jnp.log(jnp.maximum(down, 1e-30)))
    ups_before, downs_before = shifted(ups, 1, 0.0), shifted(downs, 1, 0.0)
    next_lines = shifted(lines, -1, 0.0)
    around = lines + next_lines

    xline[0:1] = diag[0:1, :nx]
    xline[1:2] = ups[0:1, :nx]
    xline[2:3] = ups_before[0:1, :nx]
    xline[3:4] = downs[0:1, :nx]
    xline[4:5] = downs_before[0:1, :nx]
    before = shifted(next_lines, 1, 0.0)
    for t in range(nt):
        cols = slice(t * LANES, (t + 1) * LANES)
        xface[0, t:t + 1] = before[0:1, cols]
        xface[1, t:t + 1] = next_lines[0:1, cols]

    def own(values, which, start):
        shift = lax.rem(length - start, length)
        return pltpu.roll(values, shift, 1)[which:which + 1]

    def passes(which, start, count):
        u0, d0 = own(ups_before, which, start)[:, 0:1], own(downs_before, which, start)
        u1, d1 = own(ups, which, start), own(downs, which, start)[:, count - 1:count]
        return u1, u0, d1, jnp.exp(jnp.minimum(u1 - u0, 0.0)), jnp.exp(jnp.minimum(d1 - d0, 0.0))

    def columns(given):
        filled = [a[:, :LANES] for a in given] + [jnp.zeros((LANES - len(given), LANES), f32)]
        return jnp.transpose(jnp.concatenate(filled, axis=0))

    z0 = col * zc
    zsums, _, _, onward, backward = passes(2, z0, zc)
    at = lax.broadcasted_iota(jnp.int32, (1, length), 1)
    zdiag = own(diag, 2, z0)
    over = jnp.where(at == zc - 1, zdiag, own(inverse, 2, z0))
    into = jnp.where(at == 0, 0.0, own(here, 2, z0) * over)
    low_end = zdiag[:, 0:1] * jnp.exp(jnp.minimum(zsums - zsums[:, 0:1], 0.0))
    scale = WEIGHT * STEP
    turned = columns([scale * over, into, scale * low_end, own(down, 2, z0), onward, backward])
    for i in range(4):
        ztab[i] = lanes_of(turned[:zc, i:i + 1])
    for i in range(2):
        zpass[i] = lanes_of(turned[:zc, 4 + i:5 + i])

    y0 = row * yc
    sums, up_first, down_last, onward, backward = passes(1, y0, yc)
    ky, kyn, kya = own(lines, 1, y0), own(next_lines, 1, y0), own(around, 1, y0)
    turned = columns([ky, kyn, 1.0 / scale - kya, onward, backward])
    yface[0] = lanes_of(turned[:yc, 0:1])
    yface[1] = lanes_of(turned[:yc, 1:2])
    ypass[0] = lanes_of(turned[:yc, 3:4])
    ypass[1] = lanes_of(turned[:yc, 4:5])
    ycoef = lanes_of(turned[:yc, 2:3])
    for t in range(nt):
        coef[t] = ycoef - around[0:1, t * LANES:(t + 1) * LANES]
    block = block_of_inverse(own(diag, 1, y0)[:, :LANES], sums[:, :LANES], LANES)[:yc, :yc]
    high, low = split(block)
    ym[...] = jnp.concatenate([high, high, low], axis=1)
    for other in range(nr):
        last, first = (other + 1) * yc - 1, other * yc
        value = jnp.exp(jnp.minimum(up_first - ups[1:2, last:last + 1], 0.0))
        weights[0, other:other + 1] = lanes_of(value)
        value = jnp.exp(jnp.minimum(downs_before[1:2, first:first + 1] - down_last, 0.0))
        weights[1, other:other + 1] = lanes_of(value)

    def rea_copy(k, t):
        rows = pl.ds(pl.multiple_of(k * 8, 8), 8)
        return pltpu.make_async_copy(
            rea_ref.at[:, rows, pl.ds(t * LANES, LANES)], base.at[t, :, rows], rea_sem.at[k, t]
        )

    def start_rea(i, _):
        k = lax.rem(i + 1, nk)
        for t in range(nt):
            rea_copy(k, t).start()
        return 0

    lax.fori_loop(0, nk, start_rea, 0)
    for copy in u_copies:
        copy.wait()

    def take_edges(z, _):
        for t in range(nt):
            edges[0, t, pl.ds(z, 1)] = u[t, z, 8 + yc - 1:8 + yc]
            edges[1, t, pl.ds(z, 1)] = u[t, z, 8:9]
        return 0

    lax.fori_loop(0, zc, take_edges, 0, unroll=4 if zc % 4 == 0 else 1)
    pl.semaphore_wait(barrier, nr - 1 + has_low.astype(jnp.int32) + has_high.astype(jnp.int32))

    def halo(side):
        return pltpu.make_async_remote_copy(
            src_ref=edges.at[side], dst_ref=yhalo.at[side],
            send_sem=hsend.at[side], recv_sem=hrecv.at[side],
            device_id=(row + 1 - 2 * side, col), device_id_type=MESH,
        )

    for side, to in ((0, up_row), (1, down_row)):
        @pl.when(to)
        def _():
            halo(side).start()

    def z_copy(side, k):
        return pltpu.make_async_remote_copy(
            src_ref=zsend.at[side, k], dst_ref=zbuf.at[side, k],
            send_sem=zsend_sem.at[side, k], recv_sem=zrecv_sem.at[side, k],
            device_id=(row, col + (1 - 2 * side)), device_id_type=MESH,
        )

    far = (col, nc - 1 - col)

    def relay(side, k):
        source, target = (has_low, has_high) if side == 0 else (has_high, has_low)
        at_row = zc - 1 if side == 0 else 0

        @pl.when(source)
        def _():
            z_copy(side, k).wait_recv()

        @pl.when(target)
        def _():
            through = zpass[side, at_row:at_row + 1]
            for t in range(nt):
                zsend[side, k, t] = zedge[side, k, t] + through * zbuf[side, k, t]
            z_copy(side, k).start()

    lane = lax.broadcasted_iota(jnp.int32, (8, LANES), 1)
    group = min(nt, 8)

    def first_pass(i, _):
        k = lax.rem(i + 1, nk)
        y = pl.multiple_of(k * 8, 8)
        rows = pl.ds(y, 8)
        for t in range(nt):
            rea_copy(k, t).wait()

        @pl.when(i == nk - 2)
        def _():
            for side, there in ((0, down_row), (1, up_row)):
                @pl.when(there)
                def _():
                    halo(side).wait_recv()

            def put(z, _):
                for t in range(nt):
                    u[t, z, 7:8] = yhalo[0, t, pl.ds(z, 1)]
                    u[t, z, 8 + yc:9 + yc] = yhalo[1, t, pl.ds(z, 1)]
                return 0

            lax.fori_loop(0, zc, put, 0, unroll=4 if zc % 4 == 0 else 1)

        for g in range(nt // group):
            tiles = [g * group + i for i in range(group)]

            def one(z, carried):
                tops, lows = carried
                over, into, low_end = ztab[0, pl.ds(z, 1)], ztab[1, pl.ds(z, 1)], ztab[2, pl.ds(z, 1)]
                kyd, kyu = yface[0, rows], yface[1, rows]
                middle = [u[t % nt, z, pl.ds(y + 8, 8)] for t in range(tiles[0] - 1, tiles[-1] + 2)] \
                    if group < nt else [u[t, z, pl.ds(y + 8, 8)] for t in tiles]
                from_low = [pltpu.roll(a, 1, 1) for a in middle]
                from_high = [pltpu.roll(a, LANES - 1, 1) for a in middle]
                n, shift = len(middle), 1 if group < nt else 0
                new_tops, new_lows = [], []
                for j, t in enumerate(tiles):
                    m = j + shift
                    c = middle[m]
                    left = jnp.where(lane == 0, from_low[(m - 1) % n], from_low[m])
                    right = jnp.where(lane == LANES - 1, from_high[(m + 1) % n], from_high[m])
                    q = base[t, z, rows] * (1.0 - c * c) + coef[t, rows]
                    value = q * c + (xface[1, t:t + 1] * right + xface[0, t:t + 1] * left)
                    value = value + (kyu * u[t, z, pl.ds(y + 9, 8)] + kyd * u[t, z, pl.ds(y + 7, 8)])
                    top = over * value + into * tops[j]
                    base[t, z, rows] = top
                    new_tops.append(top)
                    new_lows.append(lows[j] + low_end * value)
                return new_tops, new_lows

            zero = [jnp.zeros((8, LANES), f32) for _ in tiles]
            tops, lows = lax.fori_loop(0, zc, one, (zero, zero), unroll=2 if zc % 2 == 0 else 1)
            for j, t in enumerate(tiles):
                zedge[0, k, t] = tops[j]
                zedge[1, k, t] = lows[j]

        for side in (0, 1):
            turn = i - 2 * far[side]

            @pl.when(turn >= 0)
            def _():
                relay(side, lax.rem(turn + 1, nk))

        return 0

    lax.fori_loop(0, nk, first_pass, 0)

    def slot_of(d):
        return 5 * ((d + 1) // 2) + 9 * (d // 2)

    def relays(slot):
        for side in (0, 1):
            d = far[side]
            turn = slot - (slot_of(d) - (nk - 1))

            @pl.when((turn >= jnp.maximum(nk - 2 * d, 0)) & (turn < nk))
            def _():
                relay(side, lax.rem(turn + 1, nk))

    per = 256 // LANES
    steps = zc // planes

    def y_solve(tiles):
        high, low = split(jnp.concatenate(tiles, axis=1))
        return dot(ym[...], jnp.concatenate([high, low, high], axis=0))

    def second_pass(slot, _):
        for p in range(planes):
            z = zc - 1 - (slot * planes + p)
            falling = ztab[3, pl.ds(z, 1)]
            for b in range(nt // per):
                ready = []
                for t in range(b * per, (b + 1) * per):
                    v = base[t, z] + falling * vprev[t]
                    vprev[t] = v
                    ready.append(v - u[t, z, 8:8 + yc])
                solved = y_solve(ready)
                for i in range(per):
                    t = b * per + i
                    part = solved[:, i * LANES:(i + 1) * LANES]
                    base[t, z] = part
                    ye[0, t, pl.ds(z, 1)] = part[0:1]
                    ye[1, t, pl.ds(z, 1)] = part[yc - 1:yc]
        relays(slot)
        return 0

    lax.fori_loop(0, steps, second_pass, 0)

    def y_copy(side, other, slot):
        return pltpu.make_async_remote_copy(
            src_ref=ye.at[1 - side], dst_ref=ybuf.at[side, slot],
            send_sem=ysend_sem.at[side, other], recv_sem=yrecv_sem.at[side, slot],
            device_id=(other, col), device_id_type=MESH,
        )

    for other in range(nr):
        @pl.when(other > row)
        def _():
            y_copy(0, other, row).start()

        @pl.when(other < row)
        def _():
            y_copy(1, other, row).start()

    nb, bx = xw.shape[0], xw.shape[2]
    for b in range(nb):
        cols = slice(b * bx, (b + 1) * bx)
        first, last = b * bx, (b + 1) * bx - 1
        high, low = split(block_of_inverse(xline[0:1, cols], xline[1:2, cols], bx) * (1.0 / WEIGHT))
        xw[b, 0:bx] = high
        xw[b, bx:2 * bx] = high
        xw[b, 2 * bx:3 * bx] = low
        ahead = jnp.exp(xline[1:2, cols] - xline[2:3, first:first + 1])
        back = jnp.exp(xline[3:4, last:last + 1] - xline[4:5, cols])
        for i in range(bx // LANES):
            t = b * (bx // LANES) + i
            xpass[0, t:t + 1] = ahead[:, i * LANES:(i + 1) * LANES]
            xpass[1, t:t + 1] = back[:, i * LANES:(i + 1) * LANES]
        xthrough[0, b:b + 1] = lanes_of(ahead[:, bx - 1:bx])
        xthrough[1, b:b + 1] = lanes_of(back[:, 0:1])

    def third_pass(slot, _):
        zs = [slot * planes + p for p in range(planes)]
        solved = x_solve(
            lambda t: jnp.concatenate([base[t, z] for z in zs], axis=0), xw, xpass, xthrough, nt
        )
        for t in range(nt):
            for p, z in enumerate(zs):
                base[t, z] = u[t, z, 8:8 + yc] + solved[t][p * yc:(p + 1) * yc]
        relays(steps + slot)
        return 0

    lax.fori_loop(0, steps, third_pass, 0)

    def tail(slot, _):
        relays(slot)
        return 0

    most = slot_of(nc - 1) + 1
    lax.fori_loop(2 * steps, max(2 * steps, most), tail, 0)

    for k in range(2):
        for b in range(nt // per):
            tiles = [
                jnp.concatenate([zbuf[k, j, t] for j in range(nk)], axis=0)
                for t in range(b * per, (b + 1) * per)
            ]
            solved = y_solve(tiles)
            for i in range(per):
                t = b * per + i
                part = solved[:, i * LANES:(i + 1) * LANES]
                fill[k, t] = part
                esend[0, t, k:k + 1] = part[yc - 1:yc]
                esend[1, t, k:k + 1] = part[0:1]

    def e_copy(side, other, slot):
        return pltpu.make_async_remote_copy(
            src_ref=esend.at[side], dst_ref=ebuf.at[side, slot],
            send_sem=esend_sem.at[side, other], recv_sem=erecv_sem.at[side, slot],
            device_id=(other, col), device_id_type=MESH,
        )

    for other in range(nr):
        @pl.when(other > row)
        def _():
            e_copy(0, other, row).start()

        @pl.when(other < row)
        def _():
            e_copy(1, other, row).start()

    sy_ref[...] = jnp.zeros_like(sy_ref)
    for other in range(nr):
        for side, there in ((0, other < row), (1, other > row)):
            @pl.when(there)
            def _():
                y_copy(side, other, other).wait_recv()
                for t in range(nt):
                    sy_ref[side, t] += weights[side, other:other + 1] * ybuf[side, other, t]

    solved = x_solve(
        lambda t: jnp.concatenate([sy_ref[0, t], sy_ref[1, t]], axis=0), xw, xpass, xthrough, nt
    )
    for t in range(nt):
        sy_ref[0, t] = solved[t][:zc]
        sy_ref[1, t] = solved[t][zc:]

    for other in range(nr):
        for side, there in ((0, other < row), (1, other > row)):
            @pl.when(there)
            def _():
                e_copy(side, other, other).wait_recv()
                coefficients = weights[side, other:other + 1] * ypass[side]
                for t in range(nt):
                    for k in range(2):
                        fill[k, t] += coefficients * ebuf[side, other, t, k:k + 1]

    solved = x_solve(
        lambda t: jnp.concatenate([fill[0, t], fill[1, t]], axis=0), xw, xpass, xthrough, nt
    )
    for t in range(nt):
        sz_ref[0, t] = solved[t][:yc]
        sz_ref[1, t] = solved[t][yc:]

    for side, to in ((0, up_row), (1, down_row)):
        @pl.when(to)
        def _():
            halo(side).wait_send()

    for k in range(nk):
        @pl.when(has_high)
        def _():
            z_copy(0, k).wait_send()

        @pl.when(has_low)
        def _():
            z_copy(1, k).wait_send()

    for other in range(nr):
        for side, there in ((0, other > row), (1, other < row)):
            @pl.when(there)
            def _():
                y_copy(side, other, row).wait_send()
                e_copy(side, other, row).wait_send()


def finish_kernel(planes, base, sy_ref, sz_ref, zpass, ypass, out_ref):
    nt = base.shape[0]
    for p in range(planes):
        z = pl.program_id(0) * planes + p
        zb, za = zpass[0, pl.ds(z, 1)], zpass[1, pl.ds(z, 1)]
        for t in range(nt):
            value = base[t, z] + (ypass[0] * sy_ref[0, t, pl.ds(z, 1)] + ypass[1] * sy_ref[1, t, pl.ds(z, 1)])
            value = value + (zb * sz_ref[0, t] + za * sz_ref[1, t])
            out_ref[p, :, t * LANES:(t + 1) * LANES] = value


def body(u, reaction, x_faces, y_faces, z_faces, x_inverse, y_inverse, z_inverse):
    zc, yc, nx = u.shape
    nr, nc = lax.axis_size("row"), lax.axis_size("col")
    f32, bf16 = jnp.float32, jnp.bfloat16
    nt, nk = nx // LANES, yc // 8
    bx = 256
    nb = nx // bx
    planes = next(p for p in (2, 1) if zc % p == 0)
    length = -(-max(x_faces.shape[0], y_faces.shape[0], z_faces.shape[0]) // LANES) * LANES
    hbm = pl.BlockSpec(memory_space=pltpu.HBM)
    vmem = pl.BlockSpec(memory_space=pltpu.VMEM)
    there = functools.partial(pltpu.with_memory_space_constraint, memory_space=pltpu.HBM)

    def on_chip(*shape, dtype=f32):
        return pltpu.VMEM(shape, dtype)

    dma = pltpu.SemaphoreType.DMA
    base, sy, sz, zpass, ypass = pl.pallas_call(
        functools.partial(main_kernel, nr, nc, planes),
        in_specs=[hbm] * 5,
        out_specs=[vmem] * 5,
        out_shape=[
            on_chip(nt, zc, yc, LANES),
            on_chip(2, nt, zc, LANES),
            on_chip(2, nt, yc, LANES),
            on_chip(2, zc, LANES),
            on_chip(2, yc, LANES),
        ],
        scratch_shapes=[
            on_chip(3, 8, length),
            on_chip(nt, zc, yc + 16, LANES),
            on_chip(2, nt, zc, LANES),
            on_chip(2, nt, zc, LANES),
            on_chip(nt, yc, LANES),
            on_chip(2, nt, LANES),
            on_chip(2, yc, LANES),
            on_chip(4, zc, LANES),
            on_chip(8, nx),
            on_chip(nb, 3 * bx, bx, dtype=bf16),
            on_chip(2, nt, LANES),
            on_chip(2, nb, LANES),
            on_chip(yc, 3 * yc, dtype=bf16),
            on_chip(2, nr, LANES),
            on_chip(nt, yc, LANES),
            on_chip(2, nk, nt, 8, LANES),
            on_chip(2, nk, nt, 8, LANES),
            on_chip(2, nk, nt, 8, LANES),
            on_chip(2, nt, zc, LANES),
            on_chip(2, nr, nt, zc, LANES),
            on_chip(2, nt, 2, LANES),
            on_chip(2, nr, nt, 2, LANES),
            on_chip(2, nt, yc, LANES),
            dma((3,)), dma((nt,)), dma((nk, nt)), dma((2,)), dma((2,)), dma((2, nk)), dma((2, nk)),
            dma((2, nr)), dma((2, nr)), dma((2, nr)), dma((2, nr)),
        ],
        compiler_params=pltpu.CompilerParams(
            collective_id=0, has_side_effects=True, vmem_limit_bytes=MAIN_VMEM
        ),
    )(there(x_faces[None]), there(y_faces[None]), there(z_faces[None]), there(u), there(reaction))

    last = next(p for p in (4, 2, 1) if zc % p == 0)
    return pl.pallas_call(
        functools.partial(finish_kernel, last),
        grid=(zc // last,),
        in_specs=[vmem] * 5,
        out_specs=pl.BlockSpec((last, yc, nx), lambda step: (step, 0, 0)),
        out_shape=jax.ShapeDtypeStruct((zc, yc, nx), f32),
        compiler_params=pltpu.CompilerParams(vmem_limit_bytes=LAST_VMEM),
    )(base, sy, sz, zpass, ypass)


def solution(mesh):
    in_specs = (P("col", "row", None), P("col", "row", None), P(), P(), P(), P(), P(), P())
    out_specs = P("col", "row", None)
    return jax.shard_map(body, mesh=mesh, in_specs=in_specs, out_specs=out_specs, check_vma=False)
```

```python
import functools

import jax
import jax.numpy as jnp
from jax import lax
from jax.experimental import pallas as pl
from jax.experimental.pallas import tpu as pltpu
from jax.sharding import PartitionSpec as P

WEIGHT = 0.5
STEP = 1000.0
MESH = pl.DeviceIdType.MESH
LANES = 128
MAIN_VMEM = 24 * 1024 * 1024
LAST_VMEM = 12 * 1024 * 1024
FIRST_NS, HOP_NS, CHUNK_NS = 1100, 2100, 250
SECOND_NS, TABLE_NS, THIRD_NS = 280, 180, 820


def shifted(a, by, fill):
    n = a.shape[1]
    lane = lax.broadcasted_iota(jnp.int32, a.shape, 1)
    if by > 0:
        return jnp.where(lane >= by, pltpu.roll(a, by, 1), fill)
    return jnp.where(lane < n + by, pltpu.roll(a, n + by, 1), fill)


def running_sum(a):
    by = 1
    while by < a.shape[1]:
        a = a + shifted(a, by, 0.0)
        by *= 2
    return a


def ladder(couple, sign):
    p00, p01, p10, p11 = 1.0 + couple, couple, jnp.ones_like(couple), couple
    by = 1
    while by < couple.shape[1]:
        q00, q01 = shifted(p00, sign * by, 1.0), shifted(p01, sign * by, 0.0)
        q10, q11 = shifted(p10, sign * by, 0.0), shifted(p11, sign * by, 1.0)
        n00, n01 = p00 * q00 + p01 * q10, p00 * q01 + p01 * q11
        n10, n11 = p10 * q00 + p11 * q10, p10 * q01 + p11 * q11
        scale = 1.0 / (n00 + n01 + n10 + n11)
        p00, p01, p10, p11 = n00 * scale, n01 * scale, n10 * scale, n11 * scale
        by *= 2
    return p00 / p10


def as_column(line, rows):
    n = line.shape[1]
    return jnp.transpose(jnp.broadcast_to(line, (n, n)))[:rows, :rows]


def block_of_inverse(diagonal, sums, n):
    i = lax.broadcasted_iota(jnp.int32, (n, n), 0)
    j = lax.broadcasted_iota(jnp.int32, (n, n), 1)
    near = jnp.where(i >= j, diagonal[:, :n], as_column(diagonal, n))
    return near * jnp.exp(-jnp.abs(as_column(sums, n) - sums[:, :n]))


def split(a):
    high = a.astype(jnp.bfloat16)
    return high, (a - high.astype(jnp.float32)).astype(jnp.bfloat16)


def dot(a, b):
    return jnp.dot(a, b, preferred_element_type=jnp.float32)


def lanes_of(column):
    return jnp.broadcast_to(column, (column.shape[0], LANES))


def x_solve(rows_of, xw, xpass, xthrough, nt):
    nb, bx = xw.shape[0], xw.shape[2]
    per = bx // LANES
    local = []
    for b in range(nb):
        high, low = split(jnp.concatenate([rows_of(b * per + i) for i in range(per)], axis=1))
        local.append(dot(jnp.concatenate([high, low, high], axis=1), xw[b]))
    left, right = [None], [None]
    for b in range(nb - 1):
        value = lanes_of(local[b][:, bx - 1:bx])
        if b:
            value = value + left[-1] * xthrough[0, b:b + 1]
        left.append(value)
        c = nb - 1 - b
        value = lanes_of(local[c][:, 0:1])
        if b:
            value = value + right[-1] * xthrough[1, c:c + 1]
        right.append(value)
    right.reverse()
    solved = []
    for t in range(nt):
        b, i = t // per, t % per
        value = local[b][:, i * LANES:(i + 1) * LANES]
        if b:
            value = value + xpass[0, t:t + 1] * left[b]
        if b < nb - 1:
            value = value + xpass[1, t:t + 1] * right[b]
        solved.append(value)
    return solved


def main_kernel(
    nr, nc, planes, wide, xf_hbm, yf_hbm, zf_hbm, field_ref, rea_ref,
    base, sy_ref, sz_ref, zpass, ypass,
    faces, u, edges, yhalo, coef, xface, yface, ztab, xline, xw, xpass, xthrough, ym, weights,
    vprev, zedge, zsend, zbuf, pbuf, through, ye, ybuf, esend, ebuf, fill,
    face_sem, u_sem, rea_sem, hsend, hrecv, zsend_sem, zrecv_sem, psend_sem, precv_sem,
    fsend_sem, frecv_sem, ysend_sem, yrecv_sem, esend_sem, erecv_sem,
):
    row, col = lax.axis_index("row"), lax.axis_index("col")
    nt, zc, yc, _ = base.shape
    nx = nt * LANES
    nk = yc // 8
    length = faces.shape[2]
    f32 = jnp.float32

    face_copies = [
        pltpu.make_async_copy(
            a, faces.at[i, pl.ds(0, 1), pl.ds(0, a.shape[1])], face_sem.at[i]
        )
        for i, a in enumerate((xf_hbm, yf_hbm, zf_hbm))
    ]
    for i, a in enumerate((xf_hbm, yf_hbm, zf_hbm)):
        if a.shape[1] < length:
            faces[i, 0:1, a.shape[1]:] = jnp.zeros((1, length - a.shape[1]), f32)
    for copy in face_copies:
        copy.start()
    u_copies = [
        pltpu.make_async_copy(
            field_ref.at[:, :, pl.ds(t * LANES, LANES)], u.at[t, :, pl.ds(8, yc)], u_sem.at[t]
        )
        for t in range(nt)
    ]
    for copy in u_copies:
        copy.start()

    up_row, down_row = row < nr - 1, row > 0
    core, chip, chips = lax.rem(col, 2), col // 2, nc // 2
    mine, theirs = 1 - core, core
    far = jnp.where(core == 1, chip, chips - 1 - chip)
    chained, chains, fed = far > 0, far < chips - 1, far < chips - 1
    partner, following = col + 1 - 2 * core, col + 2 * (2 * core - 1)
    below, beyond = col >= 2, col < nc - 2
    barrier = pltpu.get_barrier_semaphore()
    for other in range(nr):
        @pl.when(other != row)
        def _():
            pl.semaphore_signal(barrier, inc=1, device_id=(other, col), device_id_type=MESH)

    pl.semaphore_signal(barrier, inc=1, device_id=(row, partner), device_id_type=MESH)

    @pl.when(below)
    def _():
        pl.semaphore_signal(barrier, inc=1, device_id=(row, col - 2), device_id_type=MESH)

    @pl.when(beyond)
    def _():
        pl.semaphore_signal(barrier, inc=1, device_id=(row, col + 2), device_id_type=MESH)

    vprev[...] = jnp.zeros_like(vprev)
    for side, there in ((0, down_row), (1, up_row)):
        source = chip > 0 if side == 0 else chip < chips - 1

        @pl.when(jnp.logical_not(source))
        def _():
            zbuf[side] = jnp.zeros(zbuf.shape[1:], f32)

        @pl.when(jnp.logical_not(there))
        def _():
            yhalo[side] = jnp.zeros(yhalo.shape[1:], f32)

    for copy in face_copies:
        copy.wait()

    lines = jnp.concatenate([faces[0, 0:1], faces[1, 0:1], faces[2, 0:1], jnp.zeros((5, length), f32)], axis=0)
    here = WEIGHT * STEP * lines
    above = shifted(here, -1, 0.0)
    e = ladder(here, 1)
    h = ladder(above, -1)
    pivot = above + e
    down = above / pivot
    inverse = 1.0 / pivot
    diag = 1.0 / (e + h - 1.0)
    ups = running_sum(jnp.log(jnp.maximum(here / (here + h), 1e-30)))
    downs = running_sum(jnp.log(jnp.maximum(down, 1e-30)))
    ups_before, downs_before = shifted(ups, 1, 0.0), shifted(downs, 1, 0.0)
    next_lines = shifted(lines, -1, 0.0)
    around = lines + next_lines

    xline[0:1] = diag[0:1, :nx]
    xline[1:2] = ups[0:1, :nx]
    xline[2:3] = ups_before[0:1, :nx]
    xline[3:4] = downs[0:1, :nx]
    xline[4:5] = downs_before[0:1, :nx]
    before = shifted(next_lines, 1, 0.0)
    for t in range(nt):
        cols = slice(t * LANES, (t + 1) * LANES)
        xface[0, t:t + 1] = before[0:1, cols]
        xface[1, t:t + 1] = next_lines[0:1, cols]

    def own(values, which, start):
        shift = lax.rem(length - start, length)
        return pltpu.roll(values, shift, 1)[which:which + 1]

    def passes(which, start, count):
        u0, d0 = own(ups_before, which, start)[:, 0:1], own(downs_before, which, start)
        u1, d1 = own(ups, which, start), own(downs, which, start)[:, count - 1:count]
        return u1, u0, d1, jnp.exp(jnp.minimum(u1 - u0, 0.0)), jnp.exp(jnp.minimum(d1 - d0, 0.0))

    def columns(given):
        filled = [a[:, :LANES] for a in given] + [jnp.zeros((LANES - len(given), LANES), f32)]
        return jnp.transpose(jnp.concatenate(filled, axis=0))

    z0 = col * zc
    zsums, _, _, onward, backward = passes(2, z0, zc)
    at = lax.broadcasted_iota(jnp.int32, (1, length), 1)
    zdiag = own(diag, 2, z0)
    over = jnp.where(at == zc - 1, zdiag, own(inverse, 2, z0))
    into = jnp.where(at == 0, 0.0, own(here, 2, z0) * over)
    low_end = zdiag[:, 0:1] * jnp.exp(jnp.minimum(zsums - zsums[:, 0:1], 0.0))
    scale = WEIGHT * STEP
    turned = columns([scale * over, into, scale * low_end, own(down, 2, z0), onward, backward])
    for i in range(4):
        ztab[i] = lanes_of(turned[:zc, i:i + 1])
    for i in range(2):
        zpass[i] = lanes_of(turned[:zc, 4 + i:5 + i])
    _, _, _, ponward, pbackward = passes(2, partner * zc, zc)
    here_on = jnp.where(core == 1, onward[:, zc - 1:zc], backward[:, 0:1])
    first_on = jnp.where(core == 1, ponward[:, zc - 1:zc], pbackward[:, 0:1])
    for i, value in enumerate((here_on, first_on, here_on * first_on)):
        through[i:i + 1] = lanes_of(value)

    y0 = row * yc
    sums, up_first, down_last, onward, backward = passes(1, y0, yc)
    ky, kyn, kya = own(lines, 1, y0), own(next_lines, 1, y0), own(around, 1, y0)
    turned = columns([ky, kyn, 1.0 / scale - kya, onward, backward])
    yface[0] = lanes_of(turned[:yc, 0:1])
    yface[1] = lanes_of(turned[:yc, 1:2])
    ypass[0] = lanes_of(turned[:yc, 3:4])
    ypass[1] = lanes_of(turned[:yc, 4:5])
    ycoef = lanes_of(turned[:yc, 2:3])
    for t in range(nt):
        coef[t] = ycoef - around[0:1, t * LANES:(t + 1) * LANES]
    block = block_of_inverse(own(diag, 1, y0)[:, :LANES], sums[:, :LANES], LANES)[:yc, :yc]
    high, low = split(block)
    ym[0:yc] = jnp.concatenate([high, high], axis=1)
    ym[yc:2 * yc] = jnp.concatenate([low, jnp.zeros_like(low)], axis=1)
    for other in range(nr):
        last, first = (other + 1) * yc - 1, other * yc
        value = jnp.exp(jnp.minimum(up_first - ups[1:2, last:last + 1], 0.0))
        weights[0, other:other + 1] = lanes_of(value)
        value = jnp.exp(jnp.minimum(downs_before[1:2, first:first + 1] - down_last, 0.0))
        weights[1, other:other + 1] = lanes_of(value)

    def rea_copy(k, t):
        rows = pl.ds(pl.multiple_of(k * 8, 8), 8)
        return pltpu.make_async_copy(
            rea_ref.at[:, rows, pl.ds(t * LANES, LANES)], base.at[t, :, rows], rea_sem.at[k, t]
        )

    def start_rea(i, _):
        k = lax.rem(i + 1, nk)
        for t in range(nt):
            rea_copy(k, t).start()
        return 0

    lax.fori_loop(0, nk, start_rea, 0)
    for copy in u_copies:
        copy.wait()

    def take_edges(z, _):
        for t in range(nt):
            edges[0, t, pl.ds(z, 1)] = u[t, z, 8 + yc - 1:8 + yc]
            edges[1, t, pl.ds(z, 1)] = u[t, z, 8:9]
        return 0

    lax.fori_loop(0, zc, take_edges, 0, unroll=4 if zc % 4 == 0 else 1)
    pl.semaphore_wait(barrier, nr + below.astype(jnp.int32) + beyond.astype(jnp.int32))

    def halo(side):
        return pltpu.make_async_remote_copy(
            src_ref=edges.at[side], dst_ref=yhalo.at[side],
            send_sem=hsend.at[side], recv_sem=hrecv.at[side],
            device_id=(row + 1 - 2 * side, col), device_id_type=MESH,
        )

    for side, to in ((0, up_row), (1, down_row)):
        @pl.when(to)
        def _():
            halo(side).start()

    def pair_copy(k):
        return pltpu.make_async_remote_copy(
            src_ref=zedge.at[theirs, k], dst_ref=pbuf.at[k],
            send_sem=psend_sem.at[k], recv_sem=precv_sem.at[k],
            device_id=(row, partner), device_id_type=MESH,
        )

    def chain_copy(k):
        return pltpu.make_async_remote_copy(
            src_ref=zsend.at[k], dst_ref=zbuf.at[mine, k],
            send_sem=zsend_sem.at[k], recv_sem=zrecv_sem.at[k],
            device_id=(row, following), device_id_type=MESH,
        )

    def forward_copy(k):
        return pltpu.make_async_remote_copy(
            src_ref=zbuf.at[mine, k], dst_ref=zbuf.at[mine, k],
            send_sem=fsend_sem.at[k], recv_sem=frecv_sem.at[k],
            device_id=(row, partner), device_id_type=MESH,
        )

    def relay(k):
        pair_copy(k).wait_recv()

        @pl.when(chained)
        def _():
            chain_copy(k).wait_recv()
            forward_copy(k).start()

        @pl.when(chains)
        def _():
            own_on, both_on = through[0:1], through[2:3]
            for t in range(nt):
                value = zedge[mine, k, t] + own_on * pbuf[k, t]
                zsend[k, t] = value + both_on * zbuf[mine, k, t]
            chain_copy(k).start()

    def chunk_at(j):
        return lax.rem(j + 1, nk)

    lag = (5 * far + 1) // 2

    lane = lax.broadcasted_iota(jnp.int32, (8, LANES), 1)
    group = min(nt, 8)

    long = next(n for n in (16, 8, 4, 2, 1) if zc % n == 0)

    def first_pass(i, _):
        k = lax.rem(i + 1, nk)
        y = pl.multiple_of(k * 8, 8)
        rows = pl.ds(y, 8)
        for t in range(nt):
            rea_copy(k, t).wait()

        @pl.when(i == nk - 2)
        def _():
            for side, there in ((0, down_row), (1, up_row)):
                @pl.when(there)
                def _():
                    halo(side).wait_recv()

            def put(z, _):
                for t in range(nt):
                    u[t, z, 7:8] = yhalo[0, t, pl.ds(z, 1)]
                    u[t, z, 8 + yc:9 + yc] = yhalo[1, t, pl.ds(z, 1)]
                return 0

            lax.fori_loop(0, zc, put, 0, unroll=4 if zc % 4 == 0 else 1)

        for g in range(nt // group):
            tiles = [g * group + i for i in range(group)]

            def one(z, carried):
                tops, lows = carried
                over, into, low_end = ztab[0, pl.ds(z, 1)], ztab[1, pl.ds(z, 1)], ztab[2, pl.ds(z, 1)]
                kyd, kyu = yface[0, rows], yface[1, rows]
                middle = [u[t % nt, z, pl.ds(y + 8, 8)] for t in range(tiles[0] - 1, tiles[-1] + 2)] \
                    if group < nt else [u[t, z, pl.ds(y + 8, 8)] for t in tiles]
                from_low = [pltpu.roll(a, 1, 1) for a in middle]
                from_high = [pltpu.roll(a, LANES - 1, 1) for a in middle]
                n, shift = len(middle), 1 if group < nt else 0
                new_tops, new_lows = [], []
                for j, t in enumerate(tiles):
                    m = j + shift
                    c = middle[m]
                    left = jnp.where(lane == 0, from_low[(m - 1) % n], from_low[m])
                    right = jnp.where(lane == LANES - 1, from_high[(m + 1) % n], from_high[m])
                    q = base[t, z, rows] * (1.0 - c * c) + coef[t, rows]
                    value = q * c + (xface[1, t:t + 1] * right + xface[0, t:t + 1] * left)
                    value = value + (kyu * u[t, z, pl.ds(y + 9, 8)] + kyd * u[t, z, pl.ds(y + 7, 8)])
                    top = over * value + into * tops[j]
                    base[t, z, rows] = top
                    new_tops.append(top)
                    new_lows.append(lows[j] + low_end * value)
                return new_tops, new_lows

            zero = [jnp.zeros((8, LANES), f32) for _ in tiles]
            tops, lows = lax.fori_loop(0, zc, one, (zero, zero), unroll=long)
            for j, t in enumerate(tiles):
                zedge[0, k, t] = tops[j]
                zedge[1, k, t] = lows[j]

        pair_copy(k).start()
        turn = i - 1 - lag

        @pl.when(turn >= 0)
        def _():
            relay(chunk_at(turn))

        return 0

    lax.fori_loop(0, nk, first_pass, 0)

    due = FIRST_NS + HOP_NS * far
    begun = jnp.maximum(nk - 1 - lag, 0)

    def count(now):
        ahead = (jnp.maximum(now - due + nk * CHUNK_NS, 0)) // CHUNK_NS
        return jnp.clip(ahead, begun, nk)

    def relays(since, now):
        def one(j, _):
            relay(chunk_at(j))
            return 0

        lax.fori_loop(count(since), count(now), one, 0)

    per = 256 // LANES
    steps = zc // planes

    def y_solve(tiles):
        high, low = split(jnp.concatenate(tiles, axis=1))
        both = dot(ym[...], jnp.concatenate([high, low], axis=0))
        return both[:yc] + both[yc:]

    def second_pass(slot, _):
        for p in range(planes):
            z = zc - 1 - (slot * planes + p)
            falling = ztab[3, pl.ds(z, 1)]
            for b in range(nt // per):
                ready = []
                for t in range(b * per, (b + 1) * per):
                    v = base[t, z] + falling * vprev[t]
                    vprev[t] = v
                    ready.append(v - u[t, z, 8:8 + yc])
                solved = y_solve(ready)
                for i in range(per):
                    t = b * per + i
                    part = solved[:, i * LANES:(i + 1) * LANES]
                    base[t, z] = part
                    ye[0, t, pl.ds(z, 1)] = part[0:1]
                    ye[1, t, pl.ds(z, 1)] = part[yc - 1:yc]
        relays(SECOND_NS * slot, SECOND_NS * (slot + 1))
        return 0

    lax.fori_loop(0, steps, second_pass, 0)
    now = SECOND_NS * steps

    def y_copy(side, other, slot):
        return pltpu.make_async_remote_copy(
            src_ref=ye.at[1 - side], dst_ref=ybuf.at[side, slot],
            send_sem=ysend_sem.at[side, other], recv_sem=yrecv_sem.at[side, slot],
            device_id=(other, col), device_id_type=MESH,
        )

    for other in range(nr):
        @pl.when(other > row)
        def _():
            y_copy(0, other, row).start()

        @pl.when(other < row)
        def _():
            y_copy(1, other, row).start()

    nb, bx = xw.shape[0], xw.shape[2]
    for b in range(nb):
        cols = slice(b * bx, (b + 1) * bx)
        first, last = b * bx, (b + 1) * bx - 1
        high, low = split(block_of_inverse(xline[0:1, cols], xline[1:2, cols], bx) * (1.0 / WEIGHT))
        xw[b, 0:bx] = high
        xw[b, bx:2 * bx] = high
        xw[b, 2 * bx:3 * bx] = low
        ahead = jnp.exp(xline[1:2, cols] - xline[2:3, first:first + 1])
        back = jnp.exp(xline[3:4, last:last + 1] - xline[4:5, cols])
        for i in range(bx // LANES):
            t = b * (bx // LANES) + i
            xpass[0, t:t + 1] = ahead[:, i * LANES:(i + 1) * LANES]
            xpass[1, t:t + 1] = back[:, i * LANES:(i + 1) * LANES]
        xthrough[0, b:b + 1] = lanes_of(ahead[:, bx - 1:bx])
        xthrough[1, b:b + 1] = lanes_of(back[:, 0:1])
        relays(now, now + TABLE_NS)
        now += TABLE_NS

    def third(slot):
        zs = [slot * wide + p for p in range(wide)]
        solved = x_solve(
            lambda t: jnp.concatenate([base[t, z] for z in zs], axis=0), xw, xpass, xthrough, nt
        )
        for t in range(nt):
            for p, z in enumerate(zs):
                base[t, z] = u[t, z, 8:8 + yc] + solved[t][p * yc:(p + 1) * yc]

    def third_pass(slot, _):
        third(slot)
        relays(now + THIRD_NS * slot, now + THIRD_NS * (slot + 1))
        return 0

    early = (zc // wide + 1) // 2
    lax.fori_loop(0, early, third_pass, 0)
    relays(now + THIRD_NS * early, 1 << 30)

    @pl.when(fed)
    def _():
        for k in range(nk):
            forward_copy(k).wait_recv()

    for which in range(2):
        k = theirs if which else mine
        for b in range(nt // per):
            tiles = []
            for t in range(b * per, (b + 1) * per):
                pieces = [zbuf[k, j, t] for j in range(nk)]
                if not which:
                    pieces = [pbuf[j, t] + through[1:2] * pieces[j] for j in range(nk)]
                tiles.append(jnp.concatenate(pieces, axis=0))
            solved = y_solve(tiles)
            for i in range(per):
                t = b * per + i
                part = solved[:, i * LANES:(i + 1) * LANES]
                fill[k, t] = part
                esend[0, t, pl.ds(k, 1)] = part[yc - 1:yc]
                esend[1, t, pl.ds(k, 1)] = part[0:1]

    def e_copy(side, other, slot):
        return pltpu.make_async_remote_copy(
            src_ref=esend.at[side], dst_ref=ebuf.at[side, slot],
            send_sem=esend_sem.at[side, other], recv_sem=erecv_sem.at[side, slot],
            device_id=(other, col), device_id_type=MESH,
        )

    for other in range(nr):
        @pl.when(other > row)
        def _():
            e_copy(0, other, row).start()

        @pl.when(other < row)
        def _():
            e_copy(1, other, row).start()

    def last_pass(slot, _):
        third(slot)
        return 0

    lax.fori_loop(early, zc // wide, last_pass, 0)

    sy_ref[...] = jnp.zeros_like(sy_ref)
    for other in range(nr):
        for side, there in ((0, other < row), (1, other > row)):
            @pl.when(there)
            def _():
                y_copy(side, other, other).wait_recv()
                for t in range(nt):
                    sy_ref[side, t] += weights[side, other:other + 1] * ybuf[side, other, t]

    for other in range(nr):
        for side, there in ((0, other < row), (1, other > row)):
            @pl.when(there)
            def _():
                e_copy(side, other, other).wait_recv()
                coefficients = weights[side, other:other + 1] * ypass[side]
                for t in range(nt):
                    for k in range(2):
                        fill[k, t] += coefficients * ebuf[side, other, t, k:k + 1]

    solved = x_solve(
        lambda t: jnp.concatenate([fill[0, t], fill[1, t], sy_ref[0, t], sy_ref[1, t]], axis=0),
        xw, xpass, xthrough, nt,
    )
    for t in range(nt):
        sz_ref[0, t] = solved[t][:yc]
        sz_ref[1, t] = solved[t][yc:2 * yc]
        sy_ref[0, t] = solved[t][2 * yc:2 * yc + zc]
        sy_ref[1, t] = solved[t][2 * yc + zc:]

    for side, to in ((0, up_row), (1, down_row)):
        @pl.when(to)
        def _():
            halo(side).wait_send()

    for k in range(nk):
        pair_copy(k).wait_send()

        @pl.when(chained)
        def _():
            forward_copy(k).wait_send()

        @pl.when(chains)
        def _():
            chain_copy(k).wait_send()

    for other in range(nr):
        for side, there in ((0, other > row), (1, other < row)):
            @pl.when(there)
            def _():
                y_copy(side, other, row).wait_send()
                e_copy(side, other, row).wait_send()


def finish_kernel(planes, base, sy_ref, sz_ref, zpass, ypass, out_ref, staged, sem):
    nt, zc = base.shape[0], base.shape[1]

    def out_copy(i):
        part = pl.ds(i * planes, planes)
        return pltpu.make_async_copy(staged.at[part], out_ref.at[part], sem.at[i])

    def one(i, _):
        for p in range(planes):
            z = i * planes + p
            zb, za = zpass[0, pl.ds(z, 1)], zpass[1, pl.ds(z, 1)]
            for t in range(nt):
                value = base[t, z] + (
                    ypass[0] * sy_ref[0, t, pl.ds(z, 1)] + ypass[1] * sy_ref[1, t, pl.ds(z, 1)]
                )
                value = value + (zb * sz_ref[0, t] + za * sz_ref[1, t])
                staged[z, :, t * LANES:(t + 1) * LANES] = value
        out_copy(i).start()
        return 0

    lax.fori_loop(0, zc // planes, one, 0)

    def end(i, _):
        out_copy(i).wait()
        return 0

    lax.fori_loop(0, zc // planes, end, 0)


def body(u, reaction, x_faces, y_faces, z_faces, x_inverse, y_inverse, z_inverse):
    zc, yc, nx = u.shape
    nr, nc = lax.axis_size("row"), lax.axis_size("col")
    f32, bf16 = jnp.float32, jnp.bfloat16
    nt, nk = nx // LANES, yc // 8
    bx = 256
    nb = nx // bx
    planes = next(p for p in (2, 1) if zc % p == 0)
    wide = next(p for p in (4, 2, 1) if zc % p == 0)
    length = -(-max(x_faces.shape[0], y_faces.shape[0], z_faces.shape[0]) // LANES) * LANES
    hbm = pl.BlockSpec(memory_space=pltpu.HBM)
    vmem = pl.BlockSpec(memory_space=pltpu.VMEM)
    there = functools.partial(pltpu.with_memory_space_constraint, memory_space=pltpu.HBM)

    def on_chip(*shape, dtype=f32):
        return pltpu.VMEM(shape, dtype)

    dma = pltpu.SemaphoreType.DMA
    base, sy, sz, zpass, ypass = pl.pallas_call(
        functools.partial(main_kernel, nr, nc, planes, wide),
        in_specs=[hbm] * 5,
        out_specs=[vmem] * 5,
        out_shape=[
            on_chip(nt, zc, yc, LANES),
            on_chip(2, nt, zc, LANES),
            on_chip(2, nt, yc, LANES),
            on_chip(2, zc, LANES),
            on_chip(2, yc, LANES),
        ],
        scratch_shapes=[
            on_chip(3, 8, length),
            on_chip(nt, zc, yc + 16, LANES),
            on_chip(2, nt, zc, LANES),
            on_chip(2, nt, zc, LANES),
            on_chip(nt, yc, LANES),
            on_chip(2, nt, LANES),
            on_chip(2, yc, LANES),
            on_chip(4, zc, LANES),
            on_chip(8, nx),
            on_chip(nb, 3 * bx, bx, dtype=bf16),
            on_chip(2, nt, LANES),
            on_chip(2, nb, LANES),
            on_chip(2 * yc, 2 * yc, dtype=bf16),
            on_chip(2, nr, LANES),
            on_chip(nt, yc, LANES),
            on_chip(2, nk, nt, 8, LANES),
            on_chip(nk, nt, 8, LANES),
            on_chip(2, nk, nt, 8, LANES),
            on_chip(nk, nt, 8, LANES),
            on_chip(8, LANES),
            on_chip(2, nt, zc, LANES),
            on_chip(2, nr, nt, zc, LANES),
            on_chip(2, nt, 2, LANES),
            on_chip(2, nr, nt, 2, LANES),
            on_chip(2, nt, yc, LANES),
            dma((3,)), dma((nt,)), dma((nk, nt)), dma((2,)), dma((2,)), dma((nk,)), dma((nk,)), dma((nk,)),
            dma((nk,)), dma((nk,)), dma((nk,)), dma((2, nr)), dma((2, nr)), dma((2, nr)), dma((2, nr)),
        ],
        compiler_params=pltpu.CompilerParams(
            collective_id=0, has_side_effects=True, vmem_limit_bytes=MAIN_VMEM
        ),
    )(there(x_faces[None]), there(y_faces[None]), there(z_faces[None]), there(u), there(reaction))

    last = next(p for p in (2, 1) if zc % p == 0)
    return pl.pallas_call(
        functools.partial(finish_kernel, last),
        in_specs=[vmem] * 5,
        out_specs=hbm,
        out_shape=jax.ShapeDtypeStruct((zc, yc, nx), f32),
        scratch_shapes=[on_chip(zc, yc, nx), dma((zc // last,))],
        compiler_params=pltpu.CompilerParams(vmem_limit_bytes=LAST_VMEM),
    )(base, sy, sz, zpass, ypass)


def solution(mesh):
    in_specs = (P("col", "row", None), P("col", "row", None), P(), P(), P(), P(), P(), P())
    out_specs = P("col", "row", None)
    return jax.shard_map(body, mesh=mesh, in_specs=in_specs, out_specs=out_specs, check_vma=False)
```

```python
import functools

import jax
import jax.numpy as jnp
from jax import lax
from jax.experimental import pallas as pl
from jax.experimental.pallas import tpu as pltpu
from jax.sharding import PartitionSpec as P

WEIGHT = 0.5
STEP = 1000.0
MESH = pl.DeviceIdType.MESH
LANES = 128
MAIN_VMEM = 24 * 1024 * 1024
LAST_VMEM = 12 * 1024 * 1024
FIRST_NS, HOP_NS, CHUNK_NS = 1100, 2100, 250
SECOND_NS, TABLE_NS, THIRD_NS = 280, 180, 820


def shifted(a, by, fill):
    n = a.shape[1]
    lane = lax.broadcasted_iota(jnp.int32, a.shape, 1)
    if by > 0:
        return jnp.where(lane >= by, pltpu.roll(a, by, 1), fill)
    return jnp.where(lane < n + by, pltpu.roll(a, n + by, 1), fill)


def running_sum(a):
    by = 1
    while by < a.shape[1]:
        a = a + shifted(a, by, 0.0)
        by *= 2
    return a


def ladder(couple, sign):
    p00, p01, p10, p11 = 1.0 + couple, couple, jnp.ones_like(couple), couple
    by = 1
    while by < couple.shape[1]:
        q00, q01 = shifted(p00, sign * by, 1.0), shifted(p01, sign * by, 0.0)
        q10, q11 = shifted(p10, sign * by, 0.0), shifted(p11, sign * by, 1.0)
        n00, n01 = p00 * q00 + p01 * q10, p00 * q01 + p01 * q11
        n10, n11 = p10 * q00 + p11 * q10, p10 * q01 + p11 * q11
        scale = 1.0 / (n00 + n01 + n10 + n11)
        p00, p01, p10, p11 = n00 * scale, n01 * scale, n10 * scale, n11 * scale
        by *= 2
    return p00 / p10


def as_column(line, rows):
    n = line.shape[1]
    return jnp.transpose(jnp.broadcast_to(line, (n, n)))[:rows, :rows]


def block_of_inverse(diagonal, sums, n):
    i = lax.broadcasted_iota(jnp.int32, (n, n), 0)
    j = lax.broadcasted_iota(jnp.int32, (n, n), 1)
    near = jnp.where(i >= j, diagonal[:, :n], as_column(diagonal, n))
    return near * jnp.exp(-jnp.abs(as_column(sums, n) - sums[:, :n]))


def split(a):
    high = a.astype(jnp.bfloat16)
    return high, (a - high.astype(jnp.float32)).astype(jnp.bfloat16)


def dot(a, b):
    return jnp.dot(a, b, preferred_element_type=jnp.float32)


def lanes_of(column):
    return jnp.broadcast_to(column, (column.shape[0], LANES))


def x_solve(rows_of, xw, xpass, xthrough, nt):
    nb, bx = xw.shape[0], xw.shape[2]
    per = bx // LANES
    local = []
    for b in range(nb):
        high, low = split(jnp.concatenate([rows_of(b * per + i) for i in range(per)], axis=1))
        local.append(dot(jnp.concatenate([high, low, high], axis=1), xw[b]))
    left, right = [None], [None]
    for b in range(nb - 1):
        value = lanes_of(local[b][:, bx - 1:bx])
        if b:
            value = value + left[-1] * xthrough[0, b:b + 1]
        left.append(value)
        c = nb - 1 - b
        value = lanes_of(local[c][:, 0:1])
        if b:
            value = value + right[-1] * xthrough[1, c:c + 1]
        right.append(value)
    right.reverse()
    solved = []
    for t in range(nt):
        b, i = t // per, t % per
        value = local[b][:, i * LANES:(i + 1) * LANES]
        if b:
            value = value + xpass[0, t:t + 1] * left[b]
        if b < nb - 1:
            value = value + xpass[1, t:t + 1] * right[b]
        solved.append(value)
    return solved


def main_kernel(
    nr, nc, planes, wide, u_bands, xf_hbm, yf_hbm, zf_hbm, field_ref, rea_ref,
    base, sy_ref, sz_ref, zpass, ypass,
    faces, u, edges, yhalo, coef, xface, yface, ztab, xline, xw, xpass, xthrough, ym, weights,
    vprev, zedge, zsend, zbuf, pbuf, through, ye, ybuf, esend, ebuf, fill,
    face_sem, u_sem, rea_sem, hsend, hrecv, zsend_sem, zrecv_sem, psend_sem, precv_sem,
    fsend_sem, frecv_sem, ysend_sem, yrecv_sem, esend_sem, erecv_sem,
):
    row, col = lax.axis_index("row"), lax.axis_index("col")
    nt, zc, yc, _ = base.shape
    nx = nt * LANES
    nk = yc // 8
    length = faces.shape[2]
    f32 = jnp.float32

    face_copies = [
        pltpu.make_async_copy(
            a, faces.at[i, pl.ds(0, 1), pl.ds(0, a.shape[1])], face_sem.at[i]
        )
        for i, a in enumerate((xf_hbm, yf_hbm, zf_hbm))
    ]
    for i, a in enumerate((xf_hbm, yf_hbm, zf_hbm)):
        if a.shape[1] < length:
            faces[i, 0:1, a.shape[1]:] = jnp.zeros((1, length - a.shape[1]), f32)
    for copy in face_copies:
        copy.start()
    bands = len(u_bands)
    first_row = [sum(u_bands[:i]) for i in range(bands)]

    def u_copy(i, t):
        return pltpu.make_async_copy(
            field_ref.at[:, pl.ds(first_row[i], u_bands[i]), pl.ds(t * LANES, LANES)],
            u.at[t, :, pl.ds(8 + first_row[i], u_bands[i])], u_sem.at[i, t],
        )

    def rea_copy(k, t):
        rows = pl.ds(k * 8 if isinstance(k, int) else pl.multiple_of(k * 8, 8), 8)
        return pltpu.make_async_copy(
            rea_ref.at[:, rows, pl.ds(t * LANES, LANES)], base.at[t, :, rows], rea_sem.at[k, t]
        )

    waiting = [(k + 1) % nk for k in range(nk)]
    for i in [0, bands - 1] + list(range(1, bands - 1)) if bands > 1 else [0]:
        for t in range(nt):
            u_copy(i, t).start()
        if i >= min(1, bands - 1) and i < bands - 1 or bands <= 2 and i == bands - 1:
            for k in waiting[:2]:
                for t in range(nt):
                    rea_copy(k, t).start()
            waiting = waiting[2:]
    for k in waiting:
        for t in range(nt):
            rea_copy(k, t).start()

    up_row, down_row = row < nr - 1, row > 0
    core, chip, chips = lax.rem(col, 2), col // 2, nc // 2
    mine, theirs = 1 - core, core
    far = jnp.where(core == 1, chip, chips - 1 - chip)
    chained, chains, fed = far > 0, far < chips - 1, far < chips - 1
    partner, following = col + 1 - 2 * core, col + 2 * (2 * core - 1)
    below, beyond = col >= 2, col < nc - 2
    barrier = pltpu.get_barrier_semaphore()
    for other in range(nr):
        @pl.when(other != row)
        def _():
            pl.semaphore_signal(barrier, inc=1, device_id=(other, col), device_id_type=MESH)

    pl.semaphore_signal(barrier, inc=1, device_id=(row, partner), device_id_type=MESH)

    @pl.when(below)
    def _():
        pl.semaphore_signal(barrier, inc=1, device_id=(row, col - 2), device_id_type=MESH)

    @pl.when(beyond)
    def _():
        pl.semaphore_signal(barrier, inc=1, device_id=(row, col + 2), device_id_type=MESH)

    vprev[...] = jnp.zeros_like(vprev)
    for side, there in ((0, down_row), (1, up_row)):
        source = chip > 0 if side == 0 else chip < chips - 1

        @pl.when(jnp.logical_not(source))
        def _():
            zbuf[side] = jnp.zeros(zbuf.shape[1:], f32)

        @pl.when(jnp.logical_not(there))
        def _():
            yhalo[side] = jnp.zeros(yhalo.shape[1:], f32)

    for copy in face_copies:
        copy.wait()

    lines = jnp.concatenate([faces[0, 0:1], faces[1, 0:1], faces[2, 0:1], jnp.zeros((5, length), f32)], axis=0)
    here = WEIGHT * STEP * lines
    above = shifted(here, -1, 0.0)
    e = ladder(here, 1)
    h = ladder(above, -1)
    pivot = above + e
    down = above / pivot
    inverse = 1.0 / pivot
    diag = 1.0 / (e + h - 1.0)
    ups = running_sum(jnp.log(jnp.maximum(here / (here + h), 1e-30)))
    downs = running_sum(jnp.log(jnp.maximum(down, 1e-30)))
    ups_before, downs_before = shifted(ups, 1, 0.0), shifted(downs, 1, 0.0)
    next_lines = shifted(lines, -1, 0.0)
    around = lines + next_lines

    xline[0:1] = diag[0:1, :nx]
    xline[1:2] = ups[0:1, :nx]
    xline[2:3] = ups_before[0:1, :nx]
    xline[3:4] = downs[0:1, :nx]
    xline[4:5] = downs_before[0:1, :nx]
    before = shifted(next_lines, 1, 0.0)
    for t in range(nt):
        cols = slice(t * LANES, (t + 1) * LANES)
        xface[0, t:t + 1] = before[0:1, cols]
        xface[1, t:t + 1] = next_lines[0:1, cols]

    def own(values, which, start):
        shift = lax.rem(length - start, length)
        return pltpu.roll(values, shift, 1)[which:which + 1]

    def passes(which, start, count):
        u0, d0 = own(ups_before, which, start)[:, 0:1], own(downs_before, which, start)
        u1, d1 = own(ups, which, start), own(downs, which, start)[:, count - 1:count]
        return u1, u0, d1, jnp.exp(jnp.minimum(u1 - u0, 0.0)), jnp.exp(jnp.minimum(d1 - d0, 0.0))

    def columns(given):
        filled = [a[:, :LANES] for a in given] + [jnp.zeros((LANES - len(given), LANES), f32)]
        return jnp.transpose(jnp.concatenate(filled, axis=0))

    z0 = col * zc
    zsums, _, _, onward, backward = passes(2, z0, zc)
    at = lax.broadcasted_iota(jnp.int32, (1, length), 1)
    zdiag = own(diag, 2, z0)
    over = jnp.where(at == zc - 1, zdiag, own(inverse, 2, z0))
    into = jnp.where(at == 0, 0.0, own(here, 2, z0) * over)
    low_end = zdiag[:, 0:1] * jnp.exp(jnp.minimum(zsums - zsums[:, 0:1], 0.0))
    scale = WEIGHT * STEP
    turned = columns([scale * over, into, scale * low_end, own(down, 2, z0), onward, backward])
    for i in range(4):
        ztab[i] = lanes_of(turned[:zc, i:i + 1])
    for i in range(2):
        zpass[i] = lanes_of(turned[:zc, 4 + i:5 + i])
    _, _, _, ponward, pbackward = passes(2, partner * zc, zc)
    here_on = jnp.where(core == 1, onward[:, zc - 1:zc], backward[:, 0:1])
    first_on = jnp.where(core == 1, ponward[:, zc - 1:zc], pbackward[:, 0:1])
    for i, value in enumerate((here_on, first_on, here_on * first_on)):
        through[i:i + 1] = lanes_of(value)

    y0 = row * yc
    sums, up_first, down_last, onward, backward = passes(1, y0, yc)
    ky, kyn, kya = own(lines, 1, y0), own(next_lines, 1, y0), own(around, 1, y0)
    turned = columns([ky, kyn, 1.0 / scale - kya, onward, backward])
    yface[0] = lanes_of(turned[:yc, 0:1])
    yface[1] = lanes_of(turned[:yc, 1:2])
    ypass[0] = lanes_of(turned[:yc, 3:4])
    ypass[1] = lanes_of(turned[:yc, 4:5])
    ycoef = lanes_of(turned[:yc, 2:3])
    for t in range(nt):
        coef[t] = ycoef - around[0:1, t * LANES:(t + 1) * LANES]
    block = block_of_inverse(own(diag, 1, y0)[:, :LANES], sums[:, :LANES], LANES)[:yc, :yc]
    high, low = split(block)
    ym[...] = jnp.concatenate([high, high, low], axis=1)
    for other in range(nr):
        last, first = (other + 1) * yc - 1, other * yc
        value = jnp.exp(jnp.minimum(up_first - ups[1:2, last:last + 1], 0.0))
        weights[0, other:other + 1] = lanes_of(value)
        value = jnp.exp(jnp.minimum(downs_before[1:2, first:first + 1] - down_last, 0.0))
        weights[1, other:other + 1] = lanes_of(value)

    for i in sorted({0, bands - 1}):
        for t in range(nt):
            u_copy(i, t).wait()

    def take_edges(z, _):
        for t in range(nt):
            edges[0, t, pl.ds(z, 1)] = u[t, z, 8 + yc - 1:8 + yc]
            edges[1, t, pl.ds(z, 1)] = u[t, z, 8:9]
        return 0

    lax.fori_loop(0, zc, take_edges, 0, unroll=4 if zc % 4 == 0 else 1)
    pl.semaphore_wait(barrier, nr + below.astype(jnp.int32) + beyond.astype(jnp.int32))

    def halo(side):
        return pltpu.make_async_remote_copy(
            src_ref=edges.at[side], dst_ref=yhalo.at[side],
            send_sem=hsend.at[side], recv_sem=hrecv.at[side],
            device_id=(row + 1 - 2 * side, col), device_id_type=MESH,
        )

    for side, to in ((0, up_row), (1, down_row)):
        @pl.when(to)
        def _():
            halo(side).start()

    def pair_copy(k):
        return pltpu.make_async_remote_copy(
            src_ref=zedge.at[theirs, k], dst_ref=pbuf.at[k],
            send_sem=psend_sem.at[k], recv_sem=precv_sem.at[k],
            device_id=(row, partner), device_id_type=MESH,
        )

    def chain_copy(k):
        return pltpu.make_async_remote_copy(
            src_ref=zsend.at[k], dst_ref=zbuf.at[mine, k],
            send_sem=zsend_sem.at[k], recv_sem=zrecv_sem.at[k],
            device_id=(row, following), device_id_type=MESH,
        )

    def forward_copy(k):
        return pltpu.make_async_remote_copy(
            src_ref=zbuf.at[mine, k], dst_ref=zbuf.at[mine, k],
            send_sem=fsend_sem.at[k], recv_sem=frecv_sem.at[k],
            device_id=(row, partner), device_id_type=MESH,
        )

    def relay(k):
        pair_copy(k).wait_recv()

        @pl.when(chained)
        def _():
            chain_copy(k).wait_recv()
            forward_copy(k).start()

        @pl.when(chains)
        def _():
            own_on, both_on = through[0:1], through[2:3]
            for t in range(nt):
                value = zedge[mine, k, t] + own_on * pbuf[k, t]
                zsend[k, t] = value + both_on * zbuf[mine, k, t]
            chain_copy(k).start()

    def chunk_at(j):
        return lax.rem(j + 1, nk)

    lag = (5 * far + 1) // 2

    lane = lax.broadcasted_iota(jnp.int32, (8, LANES), 1)
    group = min(nt, 8)

    long = next(n for n in (16, 8, 4, 2, 1) if zc % n == 0)

    def first_pass(i, _):
        k = lax.rem(i + 1, nk)
        y = pl.multiple_of(k * 8, 8)
        rows = pl.ds(y, 8)
        for t in range(nt):
            rea_copy(k, t).wait()

        for b in range(1, bands - 1):
            @pl.when(i == max(first_row[b] // 8 - 2, 0))
            def _():
                for t in range(nt):
                    u_copy(b, t).wait()

        @pl.when(i == nk - 2)
        def _():
            for side, there in ((0, down_row), (1, up_row)):
                @pl.when(there)
                def _():
                    halo(side).wait_recv()

            def put(z, _):
                for t in range(nt):
                    u[t, z, 7:8] = yhalo[0, t, pl.ds(z, 1)]
                    u[t, z, 8 + yc:9 + yc] = yhalo[1, t, pl.ds(z, 1)]
                return 0

            lax.fori_loop(0, zc, put, 0, unroll=4 if zc % 4 == 0 else 1)

        for g in range(nt // group):
            tiles = [g * group + i for i in range(group)]

            def one(z, carried):
                tops, lows = carried
                over, into, low_end = ztab[0, pl.ds(z, 1)], ztab[1, pl.ds(z, 1)], ztab[2, pl.ds(z, 1)]
                kyd, kyu = yface[0, rows], yface[1, rows]
                middle = [u[t % nt, z, pl.ds(y + 8, 8)] for t in range(tiles[0] - 1, tiles[-1] + 2)] \
                    if group < nt else [u[t, z, pl.ds(y + 8, 8)] for t in tiles]
                from_low = [pltpu.roll(a, 1, 1) for a in middle]
                from_high = [pltpu.roll(a, LANES - 1, 1) for a in middle]
                n, shift = len(middle), 1 if group < nt else 0
                new_tops, new_lows = [], []
                for j, t in enumerate(tiles):
                    m = j + shift
                    c = middle[m]
                    left = jnp.where(lane == 0, from_low[(m - 1) % n], from_low[m])
                    right = jnp.where(lane == LANES - 1, from_high[(m + 1) % n], from_high[m])
                    q = base[t, z, rows] * (1.0 - c * c) + coef[t, rows]
                    value = q * c + (xface[1, t:t + 1] * right + xface[0, t:t + 1] * left)
                    value = value + (kyu * u[t, z, pl.ds(y + 9, 8)] + kyd * u[t, z, pl.ds(y + 7, 8)])
                    top = over * value + into * tops[j]
                    base[t, z, rows] = top
                    new_tops.append(top)
                    new_lows.append(lows[j] + low_end * value)
                return new_tops, new_lows

            zero = [jnp.zeros((8, LANES), f32) for _ in tiles]
            tops, lows = lax.fori_loop(0, zc, one, (zero, zero), unroll=long)
            for j, t in enumerate(tiles):
                zedge[0, k, t] = tops[j]
                zedge[1, k, t] = lows[j]

        pair_copy(k).start()
        turn = i - 1 - lag

        @pl.when(turn >= 0)
        def _():
            relay(chunk_at(turn))

        return 0

    lax.fori_loop(0, nk, first_pass, 0)

    due = FIRST_NS + HOP_NS * far
    begun = jnp.maximum(nk - 1 - lag, 0)

    def count(now):
        ahead = (jnp.maximum(now - due + nk * CHUNK_NS, 0)) // CHUNK_NS
        return jnp.clip(ahead, begun, nk)

    def relays(since, now):
        def one(j, _):
            relay(chunk_at(j))
            return 0

        lax.fori_loop(count(since), count(now), one, 0)

    per = 256 // LANES
    steps = zc // planes

    def y_solve(tiles):
        high, low = split(jnp.concatenate(tiles, axis=1))
        return dot(ym[...], jnp.concatenate([high, low, high], axis=0))

    def second_pass(slot, _):
        for p in range(planes):
            z = zc - 1 - (slot * planes + p)
            falling = ztab[3, pl.ds(z, 1)]
            for b in range(nt // per):
                ready = []
                for t in range(b * per, (b + 1) * per):
                    v = base[t, z] + falling * vprev[t]
                    vprev[t] = v
                    ready.append(v - u[t, z, 8:8 + yc])
                solved = y_solve(ready)
                for i in range(per):
                    t = b * per + i
                    part = solved[:, i * LANES:(i + 1) * LANES]
                    base[t, z] = part
                    ye[0, t, pl.ds(z, 1)] = part[0:1]
                    ye[1, t, pl.ds(z, 1)] = part[yc - 1:yc]
        relays(SECOND_NS * slot, SECOND_NS * (slot + 1))
        return 0

    lax.fori_loop(0, steps, second_pass, 0)
    now = SECOND_NS * steps

    def y_copy(side, other, slot):
        return pltpu.make_async_remote_copy(
            src_ref=ye.at[1 - side], dst_ref=ybuf.at[side, slot],
            send_sem=ysend_sem.at[side, other], recv_sem=yrecv_sem.at[side, slot],
            device_id=(other, col), device_id_type=MESH,
        )

    for other in range(nr):
        @pl.when(other > row)
        def _():
            y_copy(0, other, row).start()

        @pl.when(other < row)
        def _():
            y_copy(1, other, row).start()

    nb, bx = xw.shape[0], xw.shape[2]
    for b in range(nb):
        cols = slice(b * bx, (b + 1) * bx)
        first, last = b * bx, (b + 1) * bx - 1
        high, low = split(block_of_inverse(xline[0:1, cols], xline[1:2, cols], bx) * (1.0 / WEIGHT))
        xw[b, 0:bx] = high
        xw[b, bx:2 * bx] = high
        xw[b, 2 * bx:3 * bx] = low
        ahead = jnp.exp(xline[1:2, cols] - xline[2:3, first:first + 1])
        back = jnp.exp(xline[3:4, last:last + 1] - xline[4:5, cols])
        for i in range(bx // LANES):
            t = b * (bx // LANES) + i
            xpass[0, t:t + 1] = ahead[:, i * LANES:(i + 1) * LANES]
            xpass[1, t:t + 1] = back[:, i * LANES:(i + 1) * LANES]
        xthrough[0, b:b + 1] = lanes_of(ahead[:, bx - 1:bx])
        xthrough[1, b:b + 1] = lanes_of(back[:, 0:1])
        relays(now, now + TABLE_NS)
        now += TABLE_NS

    def third(slot):
        zs = [slot * wide + p for p in range(wide)]
        solved = x_solve(
            lambda t: jnp.concatenate([base[t, z] for z in zs], axis=0), xw, xpass, xthrough, nt
        )
        for t in range(nt):
            for p, z in enumerate(zs):
                base[t, z] = u[t, z, 8:8 + yc] + solved[t][p * yc:(p + 1) * yc]

    def third_pass(slot, _):
        third(slot)
        relays(now + THIRD_NS * slot, now + THIRD_NS * (slot + 1))
        return 0

    early = (zc // wide + 1) // 2
    lax.fori_loop(0, early, third_pass, 0)
    relays(now + THIRD_NS * early, 1 << 30)

    @pl.when(fed)
    def _():
        for k in range(nk):
            forward_copy(k).wait_recv()

    for which in range(2):
        k = theirs if which else mine
        for b in range(nt // per):
            tiles = []
            for t in range(b * per, (b + 1) * per):
                pieces = [zbuf[k, j, t] for j in range(nk)]
                if not which:
                    pieces = [pbuf[j, t] + through[1:2] * pieces[j] for j in range(nk)]
                tiles.append(jnp.concatenate(pieces, axis=0))
            solved = y_solve(tiles)
            for i in range(per):
                t = b * per + i
                part = solved[:, i * LANES:(i + 1) * LANES]
                fill[k, t] = part
                esend[0, t, pl.ds(k, 1)] = part[yc - 1:yc]
                esend[1, t, pl.ds(k, 1)] = part[0:1]

    def e_copy(side, other, slot):
        return pltpu.make_async_remote_copy(
            src_ref=esend.at[side], dst_ref=ebuf.at[side, slot],
            send_sem=esend_sem.at[side, other], recv_sem=erecv_sem.at[side, slot],
            device_id=(other, col), device_id_type=MESH,
        )

    for other in range(nr):
        @pl.when(other > row)
        def _():
            e_copy(0, other, row).start()

        @pl.when(other < row)
        def _():
            e_copy(1, other, row).start()

    def last_pass(slot, _):
        third(slot)
        return 0

    lax.fori_loop(early, zc // wide, last_pass, 0)

    sy_ref[...] = jnp.zeros_like(sy_ref)
    for other in range(nr):
        for side, there in ((0, other < row), (1, other > row)):
            @pl.when(there)
            def _():
                y_copy(side, other, other).wait_recv()
                for t in range(nt):
                    sy_ref[side, t] += weights[side, other:other + 1] * ybuf[side, other, t]

    for other in range(nr):
        for side, there in ((0, other < row), (1, other > row)):
            @pl.when(there)
            def _():
                e_copy(side, other, other).wait_recv()
                coefficients = weights[side, other:other + 1] * ypass[side]
                for t in range(nt):
                    for k in range(2):
                        fill[k, t] += coefficients * ebuf[side, other, t, k:k + 1]

    solved = x_solve(
        lambda t: jnp.concatenate([fill[0, t], fill[1, t], sy_ref[0, t], sy_ref[1, t]], axis=0),
        xw, xpass, xthrough, nt,
    )
    for t in range(nt):
        sz_ref[0, t] = solved[t][:yc]
        sz_ref[1, t] = solved[t][yc:2 * yc]
        sy_ref[0, t] = solved[t][2 * yc:2 * yc + zc]
        sy_ref[1, t] = solved[t][2 * yc + zc:]

    for side, to in ((0, up_row), (1, down_row)):
        @pl.when(to)
        def _():
            halo(side).wait_send()

    for k in range(nk):
        pair_copy(k).wait_send()

        @pl.when(chained)
        def _():
            forward_copy(k).wait_send()

        @pl.when(chains)
        def _():
            chain_copy(k).wait_send()

    for other in range(nr):
        for side, there in ((0, other > row), (1, other < row)):
            @pl.when(there)
            def _():
                y_copy(side, other, row).wait_send()
                e_copy(side, other, row).wait_send()


def finish_kernel(planes, base, sy_ref, sz_ref, zpass, ypass, out_ref, staged, sem):
    nt, zc = base.shape[0], base.shape[1]

    def out_copy(i):
        part = pl.ds(i * planes, planes)
        return pltpu.make_async_copy(staged.at[part], out_ref.at[part], sem.at[i])

    def one(i, _):
        for p in range(planes):
            z = i * planes + p
            zb, za = zpass[0, pl.ds(z, 1)], zpass[1, pl.ds(z, 1)]
            for t in range(nt):
                value = base[t, z] + (
                    ypass[0] * sy_ref[0, t, pl.ds(z, 1)] + ypass[1] * sy_ref[1, t, pl.ds(z, 1)]
                )
                value = value + (zb * sz_ref[0, t] + za * sz_ref[1, t])
                staged[z, :, t * LANES:(t + 1) * LANES] = value
        out_copy(i).start()
        return 0

    lax.fori_loop(0, zc // planes, one, 0)

    def end(i, _):
        out_copy(i).wait()
        return 0

    lax.fori_loop(0, zc // planes, end, 0)


def body(u, reaction, x_faces, y_faces, z_faces, x_inverse, y_inverse, z_inverse):
    zc, yc, nx = u.shape
    nr, nc = lax.axis_size("row"), lax.axis_size("col")
    f32, bf16 = jnp.float32, jnp.bfloat16
    nt, nk = nx // LANES, yc // 8
    bx = 256
    nb = nx // bx
    u_bands = [16] * (yc // 16) if yc % 16 == 0 else [yc]
    planes = next(p for p in (2, 1) if zc % p == 0)
    wide = next(p for p in (4, 2, 1) if zc % p == 0)
    length = -(-max(x_faces.shape[0], y_faces.shape[0], z_faces.shape[0]) // LANES) * LANES
    hbm = pl.BlockSpec(memory_space=pltpu.HBM)
    vmem = pl.BlockSpec(memory_space=pltpu.VMEM)
    there = functools.partial(pltpu.with_memory_space_constraint, memory_space=pltpu.HBM)

    def on_chip(*shape, dtype=f32):
        return pltpu.VMEM(shape, dtype)

    dma = pltpu.SemaphoreType.DMA
    base, sy, sz, zpass, ypass = pl.pallas_call(
        functools.partial(main_kernel, nr, nc, planes, wide, u_bands),
        in_specs=[hbm] * 5,
        out_specs=[vmem] * 5,
        out_shape=[
            on_chip(nt, zc, yc, LANES),
            on_chip(2, nt, zc, LANES),
            on_chip(2, nt, yc, LANES),
            on_chip(2, zc, LANES),
            on_chip(2, yc, LANES),
        ],
        scratch_shapes=[
            on_chip(3, 8, length),
            on_chip(nt, zc, yc + 16, LANES),
            on_chip(2, nt, zc, LANES),
            on_chip(2, nt, zc, LANES),
            on_chip(nt, yc, LANES),
            on_chip(2, nt, LANES),
            on_chip(2, yc, LANES),
            on_chip(4, zc, LANES),
            on_chip(8, nx),
            on_chip(nb, 3 * bx, bx, dtype=bf16),
            on_chip(2, nt, LANES),
            on_chip(2, nb, LANES),
            on_chip(yc, 3 * yc, dtype=bf16),
            on_chip(2, nr, LANES),
            on_chip(nt, yc, LANES),
            on_chip(2, nk, nt, 8, LANES),
            on_chip(nk, nt, 8, LANES),
            on_chip(2, nk, nt, 8, LANES),
            on_chip(nk, nt, 8, LANES),
            on_chip(8, LANES),
            on_chip(2, nt, zc, LANES),
            on_chip(2, nr, nt, zc, LANES),
            on_chip(2, nt, 2, LANES),
            on_chip(2, nr, nt, 2, LANES),
            on_chip(2, nt, yc, LANES),
            dma((3,)), dma((len(u_bands), nt)), dma((nk, nt)), dma((2,)), dma((2,)), dma((nk,)), dma((nk,)), dma((nk,)),
            dma((nk,)), dma((nk,)), dma((nk,)), dma((2, nr)), dma((2, nr)), dma((2, nr)), dma((2, nr)),
        ],
        compiler_params=pltpu.CompilerParams(
            collective_id=0, has_side_effects=True, vmem_limit_bytes=MAIN_VMEM
        ),
    )(there(x_faces[None]), there(y_faces[None]), there(z_faces[None]), there(u), there(reaction))

    last = next(p for p in (2, 1) if zc % p == 0)
    return pl.pallas_call(
        functools.partial(finish_kernel, last),
        in_specs=[vmem] * 5,
        out_specs=hbm,
        out_shape=jax.ShapeDtypeStruct((zc, yc, nx), f32),
        scratch_shapes=[on_chip(zc, yc, nx), dma((zc // last,))],
        compiler_params=pltpu.CompilerParams(vmem_limit_bytes=LAST_VMEM),
    )(base, sy, sz, zpass, ypass)


def solution(mesh):
    in_specs = (P("col", "row", None), P("col", "row", None), P(), P(), P(), P(), P(), P())
    out_specs = P("col", "row", None)
    return jax.shard_map(body, mesh=mesh, in_specs=in_specs, out_specs=out_specs, check_vma=False)
```

```python
import functools

import jax
import jax.numpy as jnp
from jax import lax
from jax.experimental import pallas as pl
from jax.experimental.pallas import tpu as pltpu
from jax.sharding import PartitionSpec as P

WEIGHT = 0.5
STEP = 1000.0
MESH = pl.DeviceIdType.MESH
LANES = 128
TOGETHER = 4
MAIN_VMEM = 32 * 1024 * 1024
LAST_VMEM = 12 * 1024 * 1024
FIRST_NS, HOP_NS, CHUNK_NS = 1100, 2100, 250
SECOND_NS, TABLE_NS, THIRD_NS = 280, 180, 820


def shifted(a, by, fill):
    n = a.shape[1]
    lane = lax.broadcasted_iota(jnp.int32, a.shape, 1)
    if by > 0:
        return jnp.where(lane >= by, pltpu.roll(a, by, 1), fill)
    return jnp.where(lane < n + by, pltpu.roll(a, n + by, 1), fill)


def running_sum(a):
    by = 1
    while by < a.shape[1]:
        a = a + shifted(a, by, 0.0)
        by *= 2
    return a


def ladder(couple, sign):
    p00, p01, p10, p11 = 1.0 + couple, couple, jnp.ones_like(couple), couple
    by = 1
    while by < couple.shape[1]:
        q00, q01 = shifted(p00, sign * by, 1.0), shifted(p01, sign * by, 0.0)
        q10, q11 = shifted(p10, sign * by, 0.0), shifted(p11, sign * by, 1.0)
        n00, n01 = p00 * q00 + p01 * q10, p00 * q01 + p01 * q11
        n10, n11 = p10 * q00 + p11 * q10, p10 * q01 + p11 * q11
        scale = 1.0 / (n00 + n01 + n10 + n11)
        p00, p01, p10, p11 = n00 * scale, n01 * scale, n10 * scale, n11 * scale
        by *= 2
    return p00 / p10


def as_column(line, rows):
    n = line.shape[1]
    return jnp.transpose(jnp.broadcast_to(line, (n, n)))[:rows, :rows]


def block_of_inverse(diagonal, sums, n):
    i = lax.broadcasted_iota(jnp.int32, (n, n), 0)
    j = lax.broadcasted_iota(jnp.int32, (n, n), 1)
    near = jnp.where(i >= j, diagonal[:, :n], as_column(diagonal, n))
    return near * jnp.exp(-jnp.abs(as_column(sums, n) - sums[:, :n]))


def split(a):
    high = a.astype(jnp.bfloat16)
    return high, (a - high.astype(jnp.float32)).astype(jnp.bfloat16)


def dot(a, b):
    return jnp.dot(a, b, preferred_element_type=jnp.float32)


def lanes_of(column):
    return jnp.broadcast_to(column, (column.shape[0], LANES))


def x_solve(rows_of, xw, xpass, xthrough, nt):
    nb, bx = xw.shape[0], xw.shape[2]
    per = bx // LANES
    local = []
    for b in range(nb):
        high, low = split(jnp.concatenate([rows_of(b * per + i) for i in range(per)], axis=1))
        local.append(dot(jnp.concatenate([high, low, high], axis=1), xw[b]))
    left, right = [None], [None]
    for b in range(nb - 1):
        value = lanes_of(local[b][:, bx - 1:bx])
        if b:
            value = value + left[-1] * xthrough[0, b:b + 1]
        left.append(value)
        c = nb - 1 - b
        value = lanes_of(local[c][:, 0:1])
        if b:
            value = value + right[-1] * xthrough[1, c:c + 1]
        right.append(value)
    right.reverse()
    solved = []
    for t in range(nt):
        b, i = t // per, t % per
        value = local[b][:, i * LANES:(i + 1) * LANES]
        if b:
            value = value + xpass[0, t:t + 1] * left[b]
        if b < nb - 1:
            value = value + xpass[1, t:t + 1] * right[b]
        solved.append(value)
    return solved


def main_kernel(
    nr, nc, planes, wide, u_bands, xf_hbm, yf_hbm, zf_hbm, field_ref, rea_ref,
    base, sy_ref, sz_ref, zpass, ypass,
    faces, u, edges, yhalo, coef, xface, yface, ztab, xline, xw, xpass, xthrough, ym, ysolve, along, weights,
    vprev, zedge, zsend, zbuf, pbuf, through, ye, ybuf, esend, ebuf, fill,
    face_sem, u_sem, rea_sem, hsend, hrecv, zsend_sem, zrecv_sem, psend_sem, precv_sem,
    fsend_sem, frecv_sem, ysend_sem, yrecv_sem, esend_sem, erecv_sem,
):
    row, col = lax.axis_index("row"), lax.axis_index("col")
    nt, zc, yc, _ = base.shape
    nx = nt * LANES
    nk = yc // 8
    length = faces.shape[2]
    f32 = jnp.float32

    face_copies = [
        pltpu.make_async_copy(
            a, faces.at[i, pl.ds(0, 1), pl.ds(0, a.shape[1])], face_sem.at[i]
        )
        for i, a in enumerate((xf_hbm, yf_hbm, zf_hbm))
    ]
    for i, a in enumerate((xf_hbm, yf_hbm, zf_hbm)):
        if a.shape[1] < length:
            faces[i, 0:1, a.shape[1]:] = jnp.zeros((1, length - a.shape[1]), f32)
    for copy in face_copies:
        copy.start()
    bands = len(u_bands)
    first_row = [sum(u_bands[:i]) for i in range(bands)]

    def u_copy(i, t):
        return pltpu.make_async_copy(
            field_ref.at[:, pl.ds(first_row[i], u_bands[i]), pl.ds(t * LANES, LANES)],
            u.at[t, :, pl.ds(8 + first_row[i], u_bands[i])], u_sem.at[i, t],
        )

    def rea_copy(k, t):
        rows = pl.ds(k * 8 if isinstance(k, int) else pl.multiple_of(k * 8, 8), 8)
        return pltpu.make_async_copy(
            rea_ref.at[:, rows, pl.ds(t * LANES, LANES)], base.at[t, :, rows], rea_sem.at[k, t]
        )

    waiting = [(k + 1) % nk for k in range(nk)]
    for i in [0, bands - 1] + list(range(1, bands - 1)) if bands > 1 else [0]:
        for t in range(nt):
            u_copy(i, t).start()
        if i >= min(1, bands - 1) and i < bands - 1 or bands <= 2 and i == bands - 1:
            for k in waiting[:2]:
                for t in range(nt):
                    rea_copy(k, t).start()
            waiting = waiting[2:]
    for k in waiting:
        for t in range(nt):
            rea_copy(k, t).start()

    up_row, down_row = row < nr - 1, row > 0
    core, chip, chips = lax.rem(col, 2), col // 2, nc // 2
    mine, theirs = 1 - core, core
    far = jnp.where(core == 1, chip, chips - 1 - chip)
    chained, chains, fed = far > 0, far < chips - 1, far < chips - 1
    partner, following = col + 1 - 2 * core, col + 2 * (2 * core - 1)
    below, beyond = col >= 2, col < nc - 2
    barrier = pltpu.get_barrier_semaphore()
    for other in range(nr):
        @pl.when(other != row)
        def _():
            pl.semaphore_signal(barrier, inc=1, device_id=(other, col), device_id_type=MESH)

    pl.semaphore_signal(barrier, inc=1, device_id=(row, partner), device_id_type=MESH)

    @pl.when(below)
    def _():
        pl.semaphore_signal(barrier, inc=1, device_id=(row, col - 2), device_id_type=MESH)

    @pl.when(beyond)
    def _():
        pl.semaphore_signal(barrier, inc=1, device_id=(row, col + 2), device_id_type=MESH)

    vprev[...] = jnp.zeros_like(vprev)
    for side, there in ((0, down_row), (1, up_row)):
        source = chip > 0 if side == 0 else chip < chips - 1

        @pl.when(jnp.logical_not(source))
        def _():
            zbuf[side] = jnp.zeros(zbuf.shape[1:], f32)

        @pl.when(jnp.logical_not(there))
        def _():
            yhalo[side] = jnp.zeros(yhalo.shape[1:], f32)

    for copy in face_copies:
        copy.wait()

    lines = jnp.concatenate([faces[0, 0:1], faces[1, 0:1], faces[2, 0:1], jnp.zeros((5, length), f32)], axis=0)
    here = WEIGHT * STEP * lines
    above = shifted(here, -1, 0.0)
    e = ladder(here, 1)
    h = ladder(above, -1)
    pivot = above + e
    down = above / pivot
    inverse = 1.0 / pivot
    diag = 1.0 / (e + h - 1.0)
    ups = running_sum(jnp.log(jnp.maximum(here / (here + h), 1e-30)))
    downs = running_sum(jnp.log(jnp.maximum(down, 1e-30)))
    ups_before, downs_before = shifted(ups, 1, 0.0), shifted(downs, 1, 0.0)
    next_lines = shifted(lines, -1, 0.0)
    around = lines + next_lines

    xline[0:1] = diag[0:1, :nx]
    xline[1:2] = ups[0:1, :nx]
    xline[2:3] = ups_before[0:1, :nx]
    xline[3:4] = downs[0:1, :nx]
    xline[4:5] = downs_before[0:1, :nx]
    before = shifted(next_lines, 1, 0.0)
    for t in range(nt):
        cols = slice(t * LANES, (t + 1) * LANES)
        xface[0, t:t + 1] = before[0:1, cols]
        xface[1, t:t + 1] = next_lines[0:1, cols]

    def own(values, which, start):
        shift = lax.rem(length - start, length)
        return pltpu.roll(values, shift, 1)[which:which + 1]

    def passes(which, start, count):
        u0, d0 = own(ups_before, which, start)[:, 0:1], own(downs_before, which, start)
        u1, d1 = own(ups, which, start), own(downs, which, start)[:, count - 1:count]
        return u1, u0, d1, jnp.exp(jnp.minimum(u1 - u0, 0.0)), jnp.exp(jnp.minimum(d1 - d0, 0.0))

    def columns(given):
        filled = [a[:, :LANES] for a in given] + [jnp.zeros((LANES - len(given), LANES), f32)]
        return jnp.transpose(jnp.concatenate(filled, axis=0))

    z0 = col * zc
    zsums, _, _, onward, backward = passes(2, z0, zc)
    at = lax.broadcasted_iota(jnp.int32, (1, length), 1)
    zdiag = own(diag, 2, z0)
    over = jnp.where(at == zc - 1, zdiag, own(inverse, 2, z0))
    into = jnp.where(at == 0, 0.0, own(here, 2, z0) * over)
    low_end = zdiag[:, 0:1] * jnp.exp(jnp.minimum(zsums - zsums[:, 0:1], 0.0))
    scale = WEIGHT * STEP
    turned = columns([scale * over, into, scale * low_end, own(down, 2, z0), onward, backward])
    for i in range(4):
        ztab[i] = lanes_of(turned[:zc, i:i + 1])
    for i in range(2):
        zpass[i] = lanes_of(turned[:zc, 4 + i:5 + i])
    _, _, _, ponward, pbackward = passes(2, partner * zc, zc)
    here_on = jnp.where(core == 1, onward[:, zc - 1:zc], backward[:, 0:1])
    first_on = jnp.where(core == 1, ponward[:, zc - 1:zc], pbackward[:, 0:1])
    for i, value in enumerate((here_on, first_on, here_on * first_on)):
        through[i:i + 1] = lanes_of(value)

    y0 = row * yc
    sums, up_first, down_last, onward, backward = passes(1, y0, yc)
    ky, kyn, kya = own(lines, 1, y0), own(next_lines, 1, y0), own(around, 1, y0)
    seg = yc // 8
    place = lax.rem(at, seg)
    yups, yups_before = own(ups, 1, y0), own(ups_before, 1, y0)
    ydowns, ydowns_before = own(downs, 1, y0), own(downs_before, 1, y0)
    begins, ends = yups_before, ydowns
    for j in range(1, seg):
        begins = jnp.where(place == j, pltpu.roll(yups_before, j, 1), begins)
        ends = jnp.where(place == seg - 1 - j, pltpu.roll(ydowns, length - j, 1), ends)

    def decay(a):
        return jnp.exp(jnp.minimum(a, 0.0))

    seg_over = jnp.where(place == seg - 1, own(diag, 1, y0), own(inverse, 1, y0))
    seg_lines = [
        seg_over,
        jnp.where(place == 0, 0.0, own(here, 1, y0) * seg_over),
        own(down, 1, y0),
        jnp.where(at < seg, 0.0, decay(yups - begins)),
        jnp.where(at >= yc - seg, 0.0, decay(ends - ydowns_before)),
    ]
    for d in (1, 2, 4):
        value = decay(yups - pltpu.roll(yups, d * seg, 1))
        seg_lines.append(jnp.where(at < d * seg, 0.0, value))
    for d in (1, 2, 4):
        value = decay(pltpu.roll(ydowns_before, length - d * seg, 1) - ydowns_before)
        seg_lines.append(jnp.where(at >= yc - d * seg, 0.0, value))
    turned = columns([ky, kyn, 1.0 / scale - kya, onward, backward] + seg_lines)
    for i in range(len(seg_lines)):
        ysolve[i] = lanes_of(turned[:yc, 5 + i:6 + i])
    yface[0] = lanes_of(turned[:yc, 0:1])
    yface[1] = lanes_of(turned[:yc, 1:2])
    ypass[0] = lanes_of(turned[:yc, 3:4])
    ypass[1] = lanes_of(turned[:yc, 4:5])
    ycoef = lanes_of(turned[:yc, 2:3])
    for t in range(nt):
        coef[t] = ycoef - around[0:1, t * LANES:(t + 1) * LANES]
    block = block_of_inverse(own(diag, 1, y0)[:, :LANES], sums[:, :LANES], LANES)[:yc, :yc]
    high, low = split(block)
    ym[...] = jnp.concatenate([high, high, low], axis=1)
    for other in range(nr):
        last, first = (other + 1) * yc - 1, other * yc
        value = jnp.exp(jnp.minimum(up_first - ups[1:2, last:last + 1], 0.0))
        weights[0, other:other + 1] = lanes_of(value)
        value = jnp.exp(jnp.minimum(downs_before[1:2, first:first + 1] - down_last, 0.0))
        weights[1, other:other + 1] = lanes_of(value)

    for i in sorted({0, bands - 1}):
        for t in range(nt):
            u_copy(i, t).wait()

    def take_edges(z, _):
        for t in range(nt):
            edges[0, t, pl.ds(z, 1)] = u[t, z, 8 + yc - 1:8 + yc]
            edges[1, t, pl.ds(z, 1)] = u[t, z, 8:9]
        return 0

    lax.fori_loop(0, zc, take_edges, 0, unroll=4 if zc % 4 == 0 else 1)
    pl.semaphore_wait(barrier, nr + below.astype(jnp.int32) + beyond.astype(jnp.int32))

    def halo(side):
        return pltpu.make_async_remote_copy(
            src_ref=edges.at[side], dst_ref=yhalo.at[side],
            send_sem=hsend.at[side], recv_sem=hrecv.at[side],
            device_id=(row + 1 - 2 * side, col), device_id_type=MESH,
        )

    for side, to in ((0, up_row), (1, down_row)):
        @pl.when(to)
        def _():
            halo(side).start()

    def pair_copy(k):
        return pltpu.make_async_remote_copy(
            src_ref=zedge.at[theirs, k], dst_ref=pbuf.at[k],
            send_sem=psend_sem.at[k], recv_sem=precv_sem.at[k],
            device_id=(row, partner), device_id_type=MESH,
        )

    def chain_copy(k):
        return pltpu.make_async_remote_copy(
            src_ref=zsend.at[k], dst_ref=zbuf.at[mine, k],
            send_sem=zsend_sem.at[k], recv_sem=zrecv_sem.at[k],
            device_id=(row, following), device_id_type=MESH,
        )

    def forward_copy(k):
        return pltpu.make_async_remote_copy(
            src_ref=zbuf.at[mine, k], dst_ref=zbuf.at[mine, k],
            send_sem=fsend_sem.at[k], recv_sem=frecv_sem.at[k],
            device_id=(row, partner), device_id_type=MESH,
        )

    def relay(k):
        pair_copy(k).wait_recv()

        @pl.when(chained)
        def _():
            chain_copy(k).wait_recv()
            forward_copy(k).start()

        @pl.when(chains)
        def _():
            own_on, both_on = through[0:1], through[2:3]
            for t in range(nt):
                value = zedge[mine, k, t] + own_on * pbuf[k, t]
                zsend[k, t] = value + both_on * zbuf[mine, k, t]
            chain_copy(k).start()

    def chunk_at(j):
        return lax.rem(j + 1, nk)

    lag = (5 * far + 1) // 2

    lane = lax.broadcasted_iota(jnp.int32, (8, LANES), 1)
    group = min(nt, 8)

    long = next(n for n in (16, 8, 4, 2, 1) if zc % n == 0)

    def first_pass(i, _):
        k = lax.rem(i + 1, nk)
        y = pl.multiple_of(k * 8, 8)
        rows = pl.ds(y, 8)
        for t in range(nt):
            rea_copy(k, t).wait()

        for b in range(1, bands - 1):
            @pl.when(i == max(first_row[b] // 8 - 2, 0))
            def _():
                for t in range(nt):
                    u_copy(b, t).wait()

        @pl.when(i == nk - 2)
        def _():
            for side, there in ((0, down_row), (1, up_row)):
                @pl.when(there)
                def _():
                    halo(side).wait_recv()

            def put(z, _):
                for t in range(nt):
                    u[t, z, 7:8] = yhalo[0, t, pl.ds(z, 1)]
                    u[t, z, 8 + yc:9 + yc] = yhalo[1, t, pl.ds(z, 1)]
                return 0

            lax.fori_loop(0, zc, put, 0, unroll=4 if zc % 4 == 0 else 1)

        for g in range(nt // group):
            tiles = [g * group + i for i in range(group)]

            def one(z, carried):
                tops, lows = carried
                over, into, low_end = ztab[0, pl.ds(z, 1)], ztab[1, pl.ds(z, 1)], ztab[2, pl.ds(z, 1)]
                kyd, kyu = yface[0, rows], yface[1, rows]
                middle = [u[t % nt, z, pl.ds(y + 8, 8)] for t in range(tiles[0] - 1, tiles[-1] + 2)] \
                    if group < nt else [u[t, z, pl.ds(y + 8, 8)] for t in tiles]
                from_low = [pltpu.roll(a, 1, 1) for a in middle]
                from_high = [pltpu.roll(a, LANES - 1, 1) for a in middle]
                n, shift = len(middle), 1 if group < nt else 0
                new_tops, new_lows = [], []
                for j, t in enumerate(tiles):
                    m = j + shift
                    c = middle[m]
                    left = jnp.where(lane == 0, from_low[(m - 1) % n], from_low[m])
                    right = jnp.where(lane == LANES - 1, from_high[(m + 1) % n], from_high[m])
                    q = base[t, z, rows] * (1.0 - c * c) + coef[t, rows]
                    value = q * c + (xface[1, t:t + 1] * right + xface[0, t:t + 1] * left)
                    value = value + (kyu * u[t, z, pl.ds(y + 9, 8)] + kyd * u[t, z, pl.ds(y + 7, 8)])
                    top = over * value + into * tops[j]
                    base[t, z, rows] = top
                    new_tops.append(top)
                    new_lows.append(lows[j] + low_end * value)
                return new_tops, new_lows

            zero = [jnp.zeros((8, LANES), f32) for _ in tiles]
            tops, lows = lax.fori_loop(0, zc, one, (zero, zero), unroll=long)
            for j, t in enumerate(tiles):
                zedge[0, k, t] = tops[j]
                zedge[1, k, t] = lows[j]

        pair_copy(k).start()
        turn = i - 1 - lag

        @pl.when(turn >= 0)
        def _():
            relay(chunk_at(turn))

        return 0

    lax.fori_loop(0, nk, first_pass, 0)

    due = FIRST_NS + HOP_NS * far
    begun = jnp.maximum(nk - 1 - lag, 0)

    def count(now):
        ahead = (jnp.maximum(now - due + nk * CHUNK_NS, 0)) // CHUNK_NS
        return jnp.clip(ahead, begun, nk)

    def relays(since, now):
        def one(j, _):
            relay(chunk_at(j))
            return 0

        lax.fori_loop(count(since), count(now), one, 0)

    per = 256 // LANES
    steps = zc // planes

    def y_solve(tiles):
        high, low = split(jnp.concatenate(tiles, axis=1))
        return dot(ym[...], jnp.concatenate([high, low, high], axis=0))

    def segments(j):
        return pl.ds(j, 8, stride=seg)

    def y_lines(lines):
        w = [[] for _ in lines]
        for j in range(seg):
            over, into = ysolve[0, segments(j)], ysolve[1, segments(j)]
            for i, (_, _, ready) in enumerate(lines):
                value = over * ready[j]
                w[i].append(value + into * w[i][-1] if j else value)
        v = [[a[-1]] for a in w]
        for j in range(seg - 2, -1, -1):
            onto = ysolve[2, segments(j)]
            for i in range(len(lines)):
                v[i].append(w[i][j] + onto * v[i][-1])
        rising, falling = [a[0] for a in v], [a[-1] for a in v]
        for k, d in enumerate((1, 2, 4)):
            up, back = ysolve[5 + k, segments(seg - 1)], ysolve[8 + k, segments(0)]
            rising = [a + up * pltpu.roll(a, d, 0) for a in rising]
            falling = [a + back * pltpu.roll(a, 8 - d, 0) for a in falling]
        rising, falling = [pltpu.roll(a, 1, 0) for a in rising], [pltpu.roll(a, 7, 0) for a in falling]
        for j in range(seg):
            up, back = ysolve[3, segments(j)], ysolve[4, segments(j)]
            for i, (t, z, _) in enumerate(lines):
                value = v[i][seg - 1 - j] + (up * rising[i] + back * falling[i])
                along[t, z, segments(j)] = value
                if j == 0:
                    ye[0, t, pl.ds(z, 1)] = value[0:1]
                if j == seg - 1:
                    ye[1, t, pl.ds(z, 1)] = value[7:8]

    def second_pass(slot, _):
        for p in range(planes):
            z = zc - 1 - (slot * planes + p)
            onto = ztab[3, pl.ds(z, 1)]
            solved = []
            for b in range(nt // (2 * per)):
                ready = []
                for t in range(b * per, (b + 1) * per):
                    v = base[t, z] + onto * vprev[t]
                    vprev[t] = v
                    ready.append(v - u[t, z, 8:8 + yc])
                solved.append(y_solve(ready))
            for g in range(nt // (2 * TOGETHER), nt // TOGETHER):
                lines = []
                for t in range(g * TOGETHER, (g + 1) * TOGETHER):
                    ready = []
                    for j in range(seg):
                        v = base[t, z, segments(j)] + onto * vprev[t, j * 8:(j + 1) * 8]
                        vprev[t, j * 8:(j + 1) * 8] = v
                        ready.append(v - u[t, z, pl.ds(8 + j, 8, stride=seg)])
                    lines.append((t, z, ready))
                y_lines(lines)
            for b, both in enumerate(solved):
                for i in range(per):
                    t = b * per + i
                    part = both[:, i * LANES:(i + 1) * LANES]
                    along[t, z] = part
                    ye[0, t, pl.ds(z, 1)] = part[0:1]
                    ye[1, t, pl.ds(z, 1)] = part[yc - 1:yc]
        relays(SECOND_NS * slot, SECOND_NS * (slot + 1))
        return 0

    lax.fori_loop(0, steps, second_pass, 0)
    now = SECOND_NS * steps

    def y_copy(side, other, slot):
        return pltpu.make_async_remote_copy(
            src_ref=ye.at[1 - side], dst_ref=ybuf.at[side, slot],
            send_sem=ysend_sem.at[side, other], recv_sem=yrecv_sem.at[side, slot],
            device_id=(other, col), device_id_type=MESH,
        )

    for other in range(nr):
        @pl.when(other > row)
        def _():
            y_copy(0, other, row).start()

        @pl.when(other < row)
        def _():
            y_copy(1, other, row).start()

    nb, bx = xw.shape[0], xw.shape[2]
    for b in range(nb):
        cols = slice(b * bx, (b + 1) * bx)
        first, last = b * bx, (b + 1) * bx - 1
        high, low = split(block_of_inverse(xline[0:1, cols], xline[1:2, cols], bx) * (1.0 / WEIGHT))
        xw[b, 0:bx] = high
        xw[b, bx:2 * bx] = high
        xw[b, 2 * bx:3 * bx] = low
        ahead = jnp.exp(xline[1:2, cols] - xline[2:3, first:first + 1])
        back = jnp.exp(xline[3:4, last:last + 1] - xline[4:5, cols])
        for i in range(bx // LANES):
            t = b * (bx // LANES) + i
            xpass[0, t:t + 1] = ahead[:, i * LANES:(i + 1) * LANES]
            xpass[1, t:t + 1] = back[:, i * LANES:(i + 1) * LANES]
        xthrough[0, b:b + 1] = lanes_of(ahead[:, bx - 1:bx])
        xthrough[1, b:b + 1] = lanes_of(back[:, 0:1])
        relays(now, now + TABLE_NS)
        now += TABLE_NS

    def third(slot):
        zs = [slot * wide + p for p in range(wide)]
        solved = x_solve(
            lambda t: jnp.concatenate([along[t, z] for z in zs], axis=0), xw, xpass, xthrough, nt
        )
        for t in range(nt):
            for p, z in enumerate(zs):
                base[t, z] = u[t, z, 8:8 + yc] + solved[t][p * yc:(p + 1) * yc]

    def third_pass(slot, _):
        third(slot)
        relays(now + THIRD_NS * slot, now + THIRD_NS * (slot + 1))
        return 0

    early = (zc // wide + 1) // 2
    lax.fori_loop(0, early, third_pass, 0)
    relays(now + THIRD_NS * early, 1 << 30)

    @pl.when(fed)
    def _():
        for k in range(nk):
            forward_copy(k).wait_recv()

    for which in range(2):
        k = theirs if which else mine
        for b in range(nt // per):
            tiles = []
            for t in range(b * per, (b + 1) * per):
                pieces = [zbuf[k, j, t] for j in range(nk)]
                if not which:
                    pieces = [pbuf[j, t] + through[1:2] * pieces[j] for j in range(nk)]
                tiles.append(jnp.concatenate(pieces, axis=0))
            solved = y_solve(tiles)
            for i in range(per):
                t = b * per + i
                part = solved[:, i * LANES:(i + 1) * LANES]
                fill[k, t] = part
                esend[0, t, pl.ds(k, 1)] = part[yc - 1:yc]
                esend[1, t, pl.ds(k, 1)] = part[0:1]

    def e_copy(side, other, slot):
        return pltpu.make_async_remote_copy(
            src_ref=esend.at[side], dst_ref=ebuf.at[side, slot],
            send_sem=esend_sem.at[side, other], recv_sem=erecv_sem.at[side, slot],
            device_id=(other, col), device_id_type=MESH,
        )

    for other in range(nr):
        @pl.when(other > row)
        def _():
            e_copy(0, other, row).start()

        @pl.when(other < row)
        def _():
            e_copy(1, other, row).start()

    def last_pass(slot, _):
        third(slot)
        return 0

    lax.fori_loop(early, zc // wide, last_pass, 0)

    sy_ref[...] = jnp.zeros_like(sy_ref)
    for other in range(nr):
        for side, there in ((0, other < row), (1, other > row)):
            @pl.when(there)
            def _():
                y_copy(side, other, other).wait_recv()
                for t in range(nt):
                    sy_ref[side, t] += weights[side, other:other + 1] * ybuf[side, other, t]

    for other in range(nr):
        for side, there in ((0, other < row), (1, other > row)):
            @pl.when(there)
            def _():
                e_copy(side, other, other).wait_recv()
                coefficients = weights[side, other:other + 1] * ypass[side]
                for t in range(nt):
                    for k in range(2):
                        fill[k, t] += coefficients * ebuf[side, other, t, k:k + 1]

    solved = x_solve(
        lambda t: jnp.concatenate([fill[0, t], fill[1, t], sy_ref[0, t], sy_ref[1, t]], axis=0),
        xw, xpass, xthrough, nt,
    )
    for t in range(nt):
        sz_ref[0, t] = solved[t][:yc]
        sz_ref[1, t] = solved[t][yc:2 * yc]
        sy_ref[0, t] = solved[t][2 * yc:2 * yc + zc]
        sy_ref[1, t] = solved[t][2 * yc + zc:]

    for side, to in ((0, up_row), (1, down_row)):
        @pl.when(to)
        def _():
            halo(side).wait_send()

    for k in range(nk):
        pair_copy(k).wait_send()

        @pl.when(chained)
        def _():
            forward_copy(k).wait_send()

        @pl.when(chains)
        def _():
            chain_copy(k).wait_send()

    for other in range(nr):
        for side, there in ((0, other > row), (1, other < row)):
            @pl.when(there)
            def _():
                y_copy(side, other, row).wait_send()
                e_copy(side, other, row).wait_send()


def finish_kernel(planes, base, sy_ref, sz_ref, zpass, ypass, out_ref, staged, sem):
    nt, zc = base.shape[0], base.shape[1]

    def out_copy(i):
        part = pl.ds(i * planes, planes)
        return pltpu.make_async_copy(staged.at[part], out_ref.at[part], sem.at[i])

    def one(i, _):
        for p in range(planes):
            z = i * planes + p
            zb, za = zpass[0, pl.ds(z, 1)], zpass[1, pl.ds(z, 1)]
            for t in range(nt):
                value = base[t, z] + (
                    ypass[0] * sy_ref[0, t, pl.ds(z, 1)] + ypass[1] * sy_ref[1, t, pl.ds(z, 1)]
                )
                value = value + (zb * sz_ref[0, t] + za * sz_ref[1, t])
                staged[z, :, t * LANES:(t + 1) * LANES] = value
        out_copy(i).start()
        return 0

    lax.fori_loop(0, zc // planes, one, 0)

    def end(i, _):
        out_copy(i).wait()
        return 0

    lax.fori_loop(0, zc // planes, end, 0)


def body(u, reaction, x_faces, y_faces, z_faces, x_inverse, y_inverse, z_inverse):
    zc, yc, nx = u.shape
    nr, nc = lax.axis_size("row"), lax.axis_size("col")
    f32, bf16 = jnp.float32, jnp.bfloat16
    nt, nk = nx // LANES, yc // 8
    bx = 256
    nb = nx // bx
    u_bands = [16] * (yc // 16) if yc % 16 == 0 else [yc]
    planes = next(p for p in (2, 1) if zc % p == 0)
    wide = next(p for p in (4, 2, 1) if zc % p == 0)
    length = -(-max(x_faces.shape[0], y_faces.shape[0], z_faces.shape[0]) // LANES) * LANES
    hbm = pl.BlockSpec(memory_space=pltpu.HBM)
    vmem = pl.BlockSpec(memory_space=pltpu.VMEM)
    there = functools.partial(pltpu.with_memory_space_constraint, memory_space=pltpu.HBM)

    def on_chip(*shape, dtype=f32):
        return pltpu.VMEM(shape, dtype)

    dma = pltpu.SemaphoreType.DMA
    base, sy, sz, zpass, ypass = pl.pallas_call(
        functools.partial(main_kernel, nr, nc, planes, wide, u_bands),
        in_specs=[hbm] * 5,
        out_specs=[vmem] * 5,
        out_shape=[
            on_chip(nt, zc, yc, LANES),
            on_chip(2, nt, zc, LANES),
            on_chip(2, nt, yc, LANES),
            on_chip(2, zc, LANES),
            on_chip(2, yc, LANES),
        ],
        scratch_shapes=[
            on_chip(3, 8, length),
            on_chip(nt, zc, yc + 16, LANES),
            on_chip(2, nt, zc, LANES),
            on_chip(2, nt, zc, LANES),
            on_chip(nt, yc, LANES),
            on_chip(2, nt, LANES),
            on_chip(2, yc, LANES),
            on_chip(4, zc, LANES),
            on_chip(8, nx),
            on_chip(nb, 3 * bx, bx, dtype=bf16),
            on_chip(2, nt, LANES),
            on_chip(2, nb, LANES),
            on_chip(yc, 3 * yc, dtype=bf16),
            on_chip(11, yc, LANES),
            on_chip(nt, zc, yc, LANES),
            on_chip(2, nr, LANES),
            on_chip(nt, yc, LANES),
            on_chip(2, nk, nt, 8, LANES),
            on_chip(nk, nt, 8, LANES),
            on_chip(2, nk, nt, 8, LANES),
            on_chip(nk, nt, 8, LANES),
            on_chip(8, LANES),
            on_chip(2, nt, zc, LANES),
            on_chip(2, nr, nt, zc, LANES),
            on_chip(2, nt, 2, LANES),
            on_chip(2, nr, nt, 2, LANES),
            on_chip(2, nt, yc, LANES),
            dma((3,)), dma((len(u_bands), nt)), dma((nk, nt)), dma((2,)), dma((2,)), dma((nk,)), dma((nk,)), dma((nk,)),
            dma((nk,)), dma((nk,)), dma((nk,)), dma((2, nr)), dma((2, nr)), dma((2, nr)), dma((2, nr)),
        ],
        compiler_params=pltpu.CompilerParams(
            collective_id=0, has_side_effects=True, vmem_limit_bytes=MAIN_VMEM
        ),
    )(there(x_faces[None]), there(y_faces[None]), there(z_faces[None]), there(u), there(reaction))

    last = next(p for p in (2, 1) if zc % p == 0)
    return pl.pallas_call(
        functools.partial(finish_kernel, last),
        in_specs=[vmem] * 5,
        out_specs=hbm,
        out_shape=jax.ShapeDtypeStruct((zc, yc, nx), f32),
        scratch_shapes=[on_chip(zc, yc, nx), dma((zc // last,))],
        compiler_params=pltpu.CompilerParams(vmem_limit_bytes=LAST_VMEM),
    )(base, sy, sz, zpass, ypass)


def solution(mesh):
    in_specs = (P("col", "row", None), P("col", "row", None), P(), P(), P(), P(), P(), P())
    out_specs = P("col", "row", None)
    return jax.shard_map(body, mesh=mesh, in_specs=in_specs, out_specs=out_specs, check_vma=False)
```

```python
import functools

import jax
import jax.numpy as jnp
from jax import lax
from jax.experimental import pallas as pl
from jax.experimental.pallas import tpu as pltpu
from jax.sharding import PartitionSpec as P

WEIGHT = 0.5
STEP = 1000.0
MESH = pl.DeviceIdType.MESH
LANES = 128
TOGETHER = 4
MAIN_VMEM = 32 * 1024 * 1024
LAST_VMEM = 12 * 1024 * 1024
FIRST_NS, HOP_NS, CHUNK_NS = 1100, 2100, 250
SECOND_NS, TABLE_NS, THIRD_NS = 330, 150, 1350


def shifted(a, by, fill):
    n = a.shape[1]
    lane = lax.broadcasted_iota(jnp.int32, a.shape, 1)
    if by > 0:
        return jnp.where(lane >= by, pltpu.roll(a, by, 1), fill)
    return jnp.where(lane < n + by, pltpu.roll(a, n + by, 1), fill)


def running_sum(a):
    by = 1
    while by < a.shape[1]:
        a = a + shifted(a, by, 0.0)
        by *= 2
    return a


def ladder(couple, sign):
    p00, p01, p10, p11 = 1.0 + couple, couple, jnp.ones_like(couple), couple
    by = 1
    while by < couple.shape[1]:
        q00, q01 = shifted(p00, sign * by, 1.0), shifted(p01, sign * by, 0.0)
        q10, q11 = shifted(p10, sign * by, 0.0), shifted(p11, sign * by, 1.0)
        n00, n01 = p00 * q00 + p01 * q10, p00 * q01 + p01 * q11
        n10, n11 = p10 * q00 + p11 * q10, p10 * q01 + p11 * q11
        scale = 1.0 / (n00 + n01 + n10 + n11)
        p00, p01, p10, p11 = n00 * scale, n01 * scale, n10 * scale, n11 * scale
        by *= 2
    return p00 / p10


def as_column(line, rows):
    n = line.shape[1]
    return jnp.transpose(jnp.broadcast_to(line, (n, n)))[:rows, :rows]


def block_of_inverse(diagonal, sums, n):
    i = lax.broadcasted_iota(jnp.int32, (n, n), 0)
    j = lax.broadcasted_iota(jnp.int32, (n, n), 1)
    near = jnp.where(i >= j, diagonal[:, :n], as_column(diagonal, n))
    return near * jnp.exp(-jnp.abs(as_column(sums, n) - sums[:, :n]))


def split(a):
    high = a.astype(jnp.bfloat16)
    return high, (a - high.astype(jnp.float32)).astype(jnp.bfloat16)


def dot(a, b):
    return jnp.dot(a, b, preferred_element_type=jnp.float32)


def lanes_of(column):
    return jnp.broadcast_to(column, (column.shape[0], LANES))


def x_solve(rows_of, xw, xpass, xthrough, nt):
    nb, bx = xw.shape[0], xw.shape[2]
    per = bx // LANES
    local = []
    for b in range(nb):
        high, low = split(jnp.concatenate([rows_of(b * per + i) for i in range(per)], axis=1))
        local.append(dot(jnp.concatenate([high, low, high], axis=1), xw[b]))
    left, right = [None], [None]
    for b in range(nb - 1):
        value = lanes_of(local[b][:, bx - 1:bx])
        if b:
            value = value + left[-1] * xthrough[0, b:b + 1]
        left.append(value)
        c = nb - 1 - b
        value = lanes_of(local[c][:, 0:1])
        if b:
            value = value + right[-1] * xthrough[1, c:c + 1]
        right.append(value)
    right.reverse()
    solved = []
    for t in range(nt):
        b, i = t // per, t % per
        value = local[b][:, i * LANES:(i + 1) * LANES]
        if b:
            value = value + xpass[0, t:t + 1] * left[b]
        if b < nb - 1:
            value = value + xpass[1, t:t + 1] * right[b]
        solved.append(value)
    return solved


def main_kernel(
    nr, nc, planes, wide, u_bands, xf_hbm, yf_hbm, zf_hbm, field_ref, rea_ref,
    base, sy_ref, sz_ref, zpass, ypass,
    faces, u, edges, yhalo, coef, xface, yface, ztab, xline, xw, xpass, xthrough, ym, ysolve, along, weights,
    vprev, zedge, zsend, zbuf, pbuf, through, ye, ybuf, esend, ebuf, fill,
    face_sem, u_sem, rea_sem, hsend, hrecv, zsend_sem, zrecv_sem, psend_sem, precv_sem,
    fsend_sem, frecv_sem, ysend_sem, yrecv_sem, esend_sem, erecv_sem,
):
    row, col = lax.axis_index("row"), lax.axis_index("col")
    nt, zc, yc, _ = base.shape
    nx = nt * LANES
    nk = yc // 8
    length = faces.shape[2]
    f32 = jnp.float32

    face_copies = [
        pltpu.make_async_copy(
            a, faces.at[i, pl.ds(0, 1), pl.ds(0, a.shape[1])], face_sem.at[i]
        )
        for i, a in enumerate((xf_hbm, yf_hbm, zf_hbm))
    ]
    for i, a in enumerate((xf_hbm, yf_hbm, zf_hbm)):
        if a.shape[1] < length:
            faces[i, 0:1, a.shape[1]:] = jnp.zeros((1, length - a.shape[1]), f32)
    for copy in face_copies:
        copy.start()
    bands = len(u_bands)
    first_row = [sum(u_bands[:i]) for i in range(bands)]

    def u_copy(i, t):
        return pltpu.make_async_copy(
            field_ref.at[:, pl.ds(first_row[i], u_bands[i]), pl.ds(t * LANES, LANES)],
            u.at[t, :, pl.ds(8 + first_row[i], u_bands[i])], u_sem.at[i, t],
        )

    def rea_copy(k, t):
        rows = pl.ds(k * 8 if isinstance(k, int) else pl.multiple_of(k * 8, 8), 8)
        return pltpu.make_async_copy(
            rea_ref.at[:, rows, pl.ds(t * LANES, LANES)], base.at[t, :, rows], rea_sem.at[k, t]
        )

    waiting = [(k + 1) % nk for k in range(nk)]
    for i in [0, bands - 1] + list(range(1, bands - 1)) if bands > 1 else [0]:
        for t in range(nt):
            u_copy(i, t).start()
        if i >= min(1, bands - 1) and i < bands - 1 or bands <= 2 and i == bands - 1:
            for k in waiting[:2]:
                for t in range(nt):
                    rea_copy(k, t).start()
            waiting = waiting[2:]
    for k in waiting:
        for t in range(nt):
            rea_copy(k, t).start()

    up_row, down_row = row < nr - 1, row > 0
    core, chip, chips = lax.rem(col, 2), col // 2, nc // 2
    mine, theirs = 1 - core, core
    far = jnp.where(core == 1, chip, chips - 1 - chip)
    chained, chains, fed = far > 0, far < chips - 1, far < chips - 1
    partner, following = col + 1 - 2 * core, col + 2 * (2 * core - 1)
    below, beyond = col >= 2, col < nc - 2
    barrier = pltpu.get_barrier_semaphore()
    for other in range(nr):
        @pl.when(other != row)
        def _():
            pl.semaphore_signal(barrier, inc=1, device_id=(other, col), device_id_type=MESH)

    pl.semaphore_signal(barrier, inc=1, device_id=(row, partner), device_id_type=MESH)

    @pl.when(below)
    def _():
        pl.semaphore_signal(barrier, inc=1, device_id=(row, col - 2), device_id_type=MESH)

    @pl.when(beyond)
    def _():
        pl.semaphore_signal(barrier, inc=1, device_id=(row, col + 2), device_id_type=MESH)

    vprev[...] = jnp.zeros_like(vprev)
    for side, there in ((0, down_row), (1, up_row)):
        source = chip > 0 if side == 0 else chip < chips - 1

        @pl.when(jnp.logical_not(source))
        def _():
            zbuf[side] = jnp.zeros(zbuf.shape[1:], f32)

        @pl.when(jnp.logical_not(there))
        def _():
            yhalo[side] = jnp.zeros(yhalo.shape[1:], f32)

    for copy in face_copies:
        copy.wait()

    lines = jnp.concatenate([faces[0, 0:1], faces[1, 0:1], faces[2, 0:1], jnp.zeros((5, length), f32)], axis=0)
    here = WEIGHT * STEP * lines
    above = shifted(here, -1, 0.0)
    e = ladder(here, 1)
    h = ladder(above, -1)
    pivot = above + e
    down = above / pivot
    inverse = 1.0 / pivot
    diag = 1.0 / (e + h - 1.0)
    ups = running_sum(jnp.log(jnp.maximum(here / (here + h), 1e-30)))
    downs = running_sum(jnp.log(jnp.maximum(down, 1e-30)))
    ups_before, downs_before = shifted(ups, 1, 0.0), shifted(downs, 1, 0.0)
    next_lines = shifted(lines, -1, 0.0)
    around = lines + next_lines

    xline[0:1] = diag[0:1, :nx]
    xline[1:2] = ups[0:1, :nx]
    xline[2:3] = ups_before[0:1, :nx]
    xline[3:4] = downs[0:1, :nx]
    xline[4:5] = downs_before[0:1, :nx]
    before = shifted(next_lines, 1, 0.0)
    for t in range(nt):
        cols = slice(t * LANES, (t + 1) * LANES)
        xface[0, t:t + 1] = before[0:1, cols]
        xface[1, t:t + 1] = next_lines[0:1, cols]

    def own(values, which, start):
        shift = lax.rem(length - start, length)
        return pltpu.roll(values, shift, 1)[which:which + 1]

    def passes(which, start, count):
        u0, d0 = own(ups_before, which, start)[:, 0:1], own(downs_before, which, start)
        u1, d1 = own(ups, which, start), own(downs, which, start)[:, count - 1:count]
        return u1, u0, d1, jnp.exp(jnp.minimum(u1 - u0, 0.0)), jnp.exp(jnp.minimum(d1 - d0, 0.0))

    def columns(given):
        filled = [a[:, :LANES] for a in given] + [jnp.zeros((LANES - len(given), LANES), f32)]
        return jnp.transpose(jnp.concatenate(filled, axis=0))

    z0 = col * zc
    zsums, _, _, onward, backward = passes(2, z0, zc)
    at = lax.broadcasted_iota(jnp.int32, (1, length), 1)
    zdiag = own(diag, 2, z0)
    over = jnp.where(at == zc - 1, zdiag, own(inverse, 2, z0))
    into = jnp.where(at == 0, 0.0, own(here, 2, z0) * over)
    low_end = zdiag[:, 0:1] * jnp.exp(jnp.minimum(zsums - zsums[:, 0:1], 0.0))
    scale = WEIGHT * STEP
    turned = columns([scale * over, into, scale * low_end, own(down, 2, z0), onward, backward])
    for i in range(4):
        ztab[i] = lanes_of(turned[:zc, i:i + 1])
    for i in range(2):
        zpass[i] = lanes_of(turned[:zc, 4 + i:5 + i])
    _, _, _, ponward, pbackward = passes(2, partner * zc, zc)
    here_on = jnp.where(core == 1, onward[:, zc - 1:zc], backward[:, 0:1])
    first_on = jnp.where(core == 1, ponward[:, zc - 1:zc], pbackward[:, 0:1])
    for i, value in enumerate((here_on, first_on, here_on * first_on)):
        through[i:i + 1] = lanes_of(value)

    y0 = row * yc
    sums, up_first, down_last, onward, backward = passes(1, y0, yc)
    ky, kyn, kya = own(lines, 1, y0), own(next_lines, 1, y0), own(around, 1, y0)
    seg = yc // 8
    place = lax.rem(at, seg)
    yups, yups_before = own(ups, 1, y0), own(ups_before, 1, y0)
    ydowns, ydowns_before = own(downs, 1, y0), own(downs_before, 1, y0)
    begins, ends = yups_before, ydowns
    for j in range(1, seg):
        begins = jnp.where(place == j, pltpu.roll(yups_before, j, 1), begins)
        ends = jnp.where(place == seg - 1 - j, pltpu.roll(ydowns, length - j, 1), ends)

    def decay(a):
        return jnp.exp(jnp.minimum(a, 0.0))

    seg_over = jnp.where(place == seg - 1, own(diag, 1, y0), own(inverse, 1, y0))
    seg_lines = [
        seg_over,
        jnp.where(place == 0, 0.0, own(here, 1, y0) * seg_over),
        own(down, 1, y0),
        jnp.where(at < seg, 0.0, decay(yups - begins)),
        jnp.where(at >= yc - seg, 0.0, decay(ends - ydowns_before)),
    ]
    for d in (1, 2, 4):
        value = decay(yups - pltpu.roll(yups, d * seg, 1))
        seg_lines.append(jnp.where(at < d * seg, 0.0, value))
    for d in (1, 2, 4):
        value = decay(pltpu.roll(ydowns_before, length - d * seg, 1) - ydowns_before)
        seg_lines.append(jnp.where(at >= yc - d * seg, 0.0, value))
    turned = columns([ky, kyn, 1.0 / scale - kya, onward, backward] + seg_lines)
    for i in range(len(seg_lines)):
        ysolve[i] = lanes_of(turned[:yc, 5 + i:6 + i])
    yface[0] = lanes_of(turned[:yc, 0:1])
    yface[1] = lanes_of(turned[:yc, 1:2])
    ypass[0] = lanes_of(turned[:yc, 3:4])
    ypass[1] = lanes_of(turned[:yc, 4:5])
    ycoef = lanes_of(turned[:yc, 2:3])
    for t in range(nt):
        coef[t] = ycoef - around[0:1, t * LANES:(t + 1) * LANES]
    block = block_of_inverse(own(diag, 1, y0)[:, :LANES], sums[:, :LANES], LANES)[:yc, :yc]
    high, low = split(block)
    ym[...] = jnp.concatenate([high, high, low], axis=1)
    for other in range(nr):
        last, first = (other + 1) * yc - 1, other * yc
        value = jnp.exp(jnp.minimum(up_first - ups[1:2, last:last + 1], 0.0))
        weights[0, other:other + 1] = lanes_of(value)
        value = jnp.exp(jnp.minimum(downs_before[1:2, first:first + 1] - down_last, 0.0))
        weights[1, other:other + 1] = lanes_of(value)

    for i in sorted({0, bands - 1}):
        for t in range(nt):
            u_copy(i, t).wait()

    def take_edges(z, _):
        for t in range(nt):
            edges[0, t, pl.ds(z, 1)] = u[t, z, 8 + yc - 1:8 + yc]
            edges[1, t, pl.ds(z, 1)] = u[t, z, 8:9]
        return 0

    lax.fori_loop(0, zc, take_edges, 0, unroll=4 if zc % 4 == 0 else 1)
    pl.semaphore_wait(barrier, nr + below.astype(jnp.int32) + beyond.astype(jnp.int32))

    def halo(side):
        return pltpu.make_async_remote_copy(
            src_ref=edges.at[side], dst_ref=yhalo.at[side],
            send_sem=hsend.at[side], recv_sem=hrecv.at[side],
            device_id=(row + 1 - 2 * side, col), device_id_type=MESH,
        )

    for side, to in ((0, up_row), (1, down_row)):
        @pl.when(to)
        def _():
            halo(side).start()

    def pair_copy(k):
        return pltpu.make_async_remote_copy(
            src_ref=zedge.at[theirs, k], dst_ref=pbuf.at[k],
            send_sem=psend_sem.at[k], recv_sem=precv_sem.at[k],
            device_id=(row, partner), device_id_type=MESH,
        )

    def chain_copy(k):
        return pltpu.make_async_remote_copy(
            src_ref=zsend.at[k], dst_ref=zbuf.at[mine, k],
            send_sem=zsend_sem.at[k], recv_sem=zrecv_sem.at[k],
            device_id=(row, following), device_id_type=MESH,
        )

    def forward_copy(k):
        return pltpu.make_async_remote_copy(
            src_ref=zbuf.at[mine, k], dst_ref=zbuf.at[mine, k],
            send_sem=fsend_sem.at[k], recv_sem=frecv_sem.at[k],
            device_id=(row, partner), device_id_type=MESH,
        )

    def relay(k):
        pair_copy(k).wait_recv()

        @pl.when(chained)
        def _():
            chain_copy(k).wait_recv()
            forward_copy(k).start()

        @pl.when(chains)
        def _():
            own_on, both_on = through[0:1], through[2:3]
            for t in range(nt):
                value = zedge[mine, k, t] + own_on * pbuf[k, t]
                zsend[k, t] = value + both_on * zbuf[mine, k, t]
            chain_copy(k).start()

    def chunk_at(j):
        return lax.rem(j + 1, nk)

    lag = (5 * far + 1) // 2

    lane = lax.broadcasted_iota(jnp.int32, (8, LANES), 1)
    group = min(nt, 8)

    long = next(n for n in (16, 8, 4, 2, 1) if zc % n == 0)

    def first_pass(i, _):
        k = lax.rem(i + 1, nk)
        y = pl.multiple_of(k * 8, 8)
        rows = pl.ds(y, 8)
        for t in range(nt):
            rea_copy(k, t).wait()

        for b in range(1, bands - 1):
            @pl.when(i == max(first_row[b] // 8 - 2, 0))
            def _():
                for t in range(nt):
                    u_copy(b, t).wait()

        @pl.when(i == nk - 2)
        def _():
            for side, there in ((0, down_row), (1, up_row)):
                @pl.when(there)
                def _():
                    halo(side).wait_recv()

            def put(z, _):
                for t in range(nt):
                    u[t, z, 7:8] = yhalo[0, t, pl.ds(z, 1)]
                    u[t, z, 8 + yc:9 + yc] = yhalo[1, t, pl.ds(z, 1)]
                return 0

            lax.fori_loop(0, zc, put, 0, unroll=4 if zc % 4 == 0 else 1)

        for g in range(nt // group):
            tiles = [g * group + i for i in range(group)]

            def one(z, carried):
                tops, lows = carried
                over, into, low_end = ztab[0, pl.ds(z, 1)], ztab[1, pl.ds(z, 1)], ztab[2, pl.ds(z, 1)]
                kyd, kyu = yface[0, rows], yface[1, rows]
                middle = [u[t % nt, z, pl.ds(y + 8, 8)] for t in range(tiles[0] - 1, tiles[-1] + 2)] \
                    if group < nt else [u[t, z, pl.ds(y + 8, 8)] for t in tiles]
                from_low = [pltpu.roll(a, 1, 1) for a in middle]
                from_high = [pltpu.roll(a, LANES - 1, 1) for a in middle]
                n, shift = len(middle), 1 if group < nt else 0
                new_tops, new_lows = [], []
                for j, t in enumerate(tiles):
                    m = j + shift
                    c = middle[m]
                    left = jnp.where(lane == 0, from_low[(m - 1) % n], from_low[m])
                    right = jnp.where(lane == LANES - 1, from_high[(m + 1) % n], from_high[m])
                    q = base[t, z, rows] * (1.0 - c * c) + coef[t, rows]
                    value = q * c + (xface[1, t:t + 1] * right + xface[0, t:t + 1] * left)
                    value = value + (kyu * u[t, z, pl.ds(y + 9, 8)] + kyd * u[t, z, pl.ds(y + 7, 8)])
                    top = over * value + into * tops[j]
                    base[t, z, rows] = top
                    new_tops.append(top)
                    new_lows.append(lows[j] + low_end * value)
                return new_tops, new_lows

            zero = [jnp.zeros((8, LANES), f32) for _ in tiles]
            tops, lows = lax.fori_loop(0, zc, one, (zero, zero), unroll=long)
            for j, t in enumerate(tiles):
                zedge[0, k, t] = tops[j]
                zedge[1, k, t] = lows[j]

        pair_copy(k).start()
        turn = i - 1 - lag

        @pl.when(turn >= 0)
        def _():
            relay(chunk_at(turn))

        return 0

    lax.fori_loop(0, nk, first_pass, 0)

    due = FIRST_NS + HOP_NS * far
    begun = jnp.maximum(nk - 1 - lag, 0)

    def count(now):
        ahead = (jnp.maximum(now - due + nk * CHUNK_NS, 0)) // CHUNK_NS
        return jnp.clip(ahead, begun, nk)

    def relays(since, now):
        def one(j, _):
            relay(chunk_at(j))
            return 0

        lax.fori_loop(count(since), count(now), one, 0)

    per = 256 // LANES
    steps = zc // planes

    def y_solve(tiles):
        high, low = split(jnp.concatenate(tiles, axis=1))
        return dot(ym[...], jnp.concatenate([high, low, high], axis=0))

    def segments(j):
        return pl.ds(j, 8, stride=seg)

    def y_lines(lines):
        w = [[] for _ in lines]
        for j in range(seg):
            over, into = ysolve[0, segments(j)], ysolve[1, segments(j)]
            for i, (_, _, ready) in enumerate(lines):
                value = over * ready[j]
                w[i].append(value + into * w[i][-1] if j else value)
        v = [[a[-1]] for a in w]
        for j in range(seg - 2, -1, -1):
            onto = ysolve[2, segments(j)]
            for i in range(len(lines)):
                v[i].append(w[i][j] + onto * v[i][-1])
        rising, falling = [a[0] for a in v], [a[-1] for a in v]
        for k, d in enumerate((1, 2, 4)):
            up, back = ysolve[5 + k, segments(seg - 1)], ysolve[8 + k, segments(0)]
            rising = [a + up * pltpu.roll(a, d, 0) for a in rising]
            falling = [a + back * pltpu.roll(a, 8 - d, 0) for a in falling]
        rising, falling = [pltpu.roll(a, 1, 0) for a in rising], [pltpu.roll(a, 7, 0) for a in falling]
        for j in range(seg):
            up, back = ysolve[3, segments(j)], ysolve[4, segments(j)]
            for i, (t, z, _) in enumerate(lines):
                value = v[i][seg - 1 - j] + (up * rising[i] + back * falling[i])
                along[t, z, segments(j)] = value
                if j == 0:
                    ye[0, t, pl.ds(z, 1)] = value[0:1]
                if j == seg - 1:
                    ye[1, t, pl.ds(z, 1)] = value[7:8]

    def second_pass(slot, _):
        for p in range(planes):
            z = zc - 1 - (slot * planes + p)
            onto = ztab[3, pl.ds(z, 1)]
            solved = []
            for b in range(nt // (2 * per)):
                ready = []
                for t in range(b * per, (b + 1) * per):
                    v = base[t, z] + onto * vprev[t]
                    vprev[t] = v
                    ready.append(v - u[t, z, 8:8 + yc])
                solved.append(y_solve(ready))
            for g in range(nt // (2 * TOGETHER), nt // TOGETHER):
                lines = []
                for t in range(g * TOGETHER, (g + 1) * TOGETHER):
                    ready = []
                    for j in range(seg):
                        v = base[t, z, segments(j)] + onto * vprev[t, j * 8:(j + 1) * 8]
                        vprev[t, j * 8:(j + 1) * 8] = v
                        ready.append(v - u[t, z, pl.ds(8 + j, 8, stride=seg)])
                    lines.append((t, z, ready))
                y_lines(lines)
            for b, both in enumerate(solved):
                for i in range(per):
                    t = b * per + i
                    part = both[:, i * LANES:(i + 1) * LANES]
                    along[t, z] = part
                    ye[0, t, pl.ds(z, 1)] = part[0:1]
                    ye[1, t, pl.ds(z, 1)] = part[yc - 1:yc]
        relays(SECOND_NS * slot, SECOND_NS * (slot + 1))
        return 0

    lax.fori_loop(0, steps, second_pass, 0)
    now = SECOND_NS * steps

    def y_copy(side, other, slot):
        return pltpu.make_async_remote_copy(
            src_ref=ye.at[1 - side], dst_ref=ybuf.at[side, slot],
            send_sem=ysend_sem.at[side, other], recv_sem=yrecv_sem.at[side, slot],
            device_id=(other, col), device_id_type=MESH,
        )

    for other in range(nr):
        @pl.when(other > row)
        def _():
            y_copy(0, other, row).start()

        @pl.when(other < row)
        def _():
            y_copy(1, other, row).start()

    nb, bx = xw.shape[0], xw.shape[2]
    for b in range(nb):
        cols = slice(b * bx, (b + 1) * bx)
        first, last = b * bx, (b + 1) * bx - 1
        high, low = split(block_of_inverse(xline[0:1, cols], xline[1:2, cols], bx) * (1.0 / WEIGHT))
        xw[b, 0:bx] = high
        xw[b, bx:2 * bx] = high
        xw[b, 2 * bx:3 * bx] = low
        ahead = jnp.exp(xline[1:2, cols] - xline[2:3, first:first + 1])
        back = jnp.exp(xline[3:4, last:last + 1] - xline[4:5, cols])
        for i in range(bx // LANES):
            t = b * (bx // LANES) + i
            xpass[0, t:t + 1] = ahead[:, i * LANES:(i + 1) * LANES]
            xpass[1, t:t + 1] = back[:, i * LANES:(i + 1) * LANES]
        xthrough[0, b:b + 1] = lanes_of(ahead[:, bx - 1:bx])
        xthrough[1, b:b + 1] = lanes_of(back[:, 0:1])
        relays(now, now + TABLE_NS)
        now += TABLE_NS

    def third(slot):
        zs = [slot * wide + p for p in range(wide)]
        solved = x_solve(
            lambda t: jnp.concatenate([along[t, z] for z in zs], axis=0), xw, xpass, xthrough, nt
        )
        for t in range(nt):
            for p, z in enumerate(zs):
                base[t, z] = u[t, z, 8:8 + yc] + solved[t][p * yc:(p + 1) * yc]

    def third_pass(slot, _):
        third(slot)
        relays(now + THIRD_NS * slot, now + THIRD_NS * (slot + 1))
        return 0

    early = (zc // wide + 1) // 2
    lax.fori_loop(0, early, third_pass, 0)
    relays(now + THIRD_NS * early, 1 << 30)

    @pl.when(fed)
    def _():
        for k in range(nk):
            forward_copy(k).wait_recv()

    for which in range(2):
        k = theirs if which else mine
        for b in range(nt // per):
            tiles = []
            for t in range(b * per, (b + 1) * per):
                pieces = [zbuf[k, j, t] for j in range(nk)]
                if not which:
                    pieces = [pbuf[j, t] + through[1:2] * pieces[j] for j in range(nk)]
                tiles.append(jnp.concatenate(pieces, axis=0))
            solved = y_solve(tiles)
            for i in range(per):
                t = b * per + i
                part = solved[:, i * LANES:(i + 1) * LANES]
                fill[k, t] = part
                esend[0, t, pl.ds(k, 1)] = part[yc - 1:yc]
                esend[1, t, pl.ds(k, 1)] = part[0:1]

    def e_copy(side, other, slot):
        return pltpu.make_async_remote_copy(
            src_ref=esend.at[side], dst_ref=ebuf.at[side, slot],
            send_sem=esend_sem.at[side, other], recv_sem=erecv_sem.at[side, slot],
            device_id=(other, col), device_id_type=MESH,
        )

    for other in range(nr):
        @pl.when(other > row)
        def _():
            e_copy(0, other, row).start()

        @pl.when(other < row)
        def _():
            e_copy(1, other, row).start()

    def last_pass(slot, _):
        third(slot)
        return 0

    lax.fori_loop(early, zc // wide, last_pass, 0)

    sy_ref[...] = jnp.zeros_like(sy_ref)
    for other in range(nr):
        for side, there in ((0, other < row), (1, other > row)):
            @pl.when(there)
            def _():
                y_copy(side, other, other).wait_recv()
                for t in range(nt):
                    sy_ref[side, t] += weights[side, other:other + 1] * ybuf[side, other, t]

    for other in range(nr):
        for side, there in ((0, other < row), (1, other > row)):
            @pl.when(there)
            def _():
                e_copy(side, other, other).wait_recv()
                coefficients = weights[side, other:other + 1] * ypass[side]
                for t in range(nt):
                    for k in range(2):
                        fill[k, t] += coefficients * ebuf[side, other, t, k:k + 1]

    solved = x_solve(
        lambda t: jnp.concatenate([fill[0, t], fill[1, t], sy_ref[0, t], sy_ref[1, t]], axis=0),
        xw, xpass, xthrough, nt,
    )
    for t in range(nt):
        sz_ref[0, t] = solved[t][:yc]
        sz_ref[1, t] = solved[t][yc:2 * yc]
        sy_ref[0, t] = solved[t][2 * yc:2 * yc + zc]
        sy_ref[1, t] = solved[t][2 * yc + zc:]

    for side, to in ((0, up_row), (1, down_row)):
        @pl.when(to)
        def _():
            halo(side).wait_send()

    for k in range(nk):
        pair_copy(k).wait_send()

        @pl.when(chained)
        def _():
            forward_copy(k).wait_send()

        @pl.when(chains)
        def _():
            chain_copy(k).wait_send()

    for other in range(nr):
        for side, there in ((0, other > row), (1, other < row)):
            @pl.when(there)
            def _():
                y_copy(side, other, row).wait_send()
                e_copy(side, other, row).wait_send()


def finish_kernel(planes, base, sy_ref, sz_ref, zpass, ypass, out_ref, staged, sem):
    nt, zc = base.shape[0], base.shape[1]

    def out_copy(i):
        part = pl.ds(i * planes, planes)
        return pltpu.make_async_copy(staged.at[part], out_ref.at[part], sem.at[i])

    def one(i, _):
        for p in range(planes):
            z = i * planes + p
            zb, za = zpass[0, pl.ds(z, 1)], zpass[1, pl.ds(z, 1)]
            for t in range(nt):
                value = base[t, z] + (
                    ypass[0] * sy_ref[0, t, pl.ds(z, 1)] + ypass[1] * sy_ref[1, t, pl.ds(z, 1)]
                )
                value = value + (zb * sz_ref[0, t] + za * sz_ref[1, t])
                staged[z, :, t * LANES:(t + 1) * LANES] = value
        out_copy(i).start()
        return 0

    lax.fori_loop(0, zc // planes, one, 0)

    def end(i, _):
        out_copy(i).wait()
        return 0

    lax.fori_loop(0, zc // planes, end, 0)


def body(u, reaction, x_faces, y_faces, z_faces, x_inverse, y_inverse, z_inverse):
    zc, yc, nx = u.shape
    nr, nc = lax.axis_size("row"), lax.axis_size("col")
    f32, bf16 = jnp.float32, jnp.bfloat16
    nt, nk = nx // LANES, yc // 8
    bx = 256
    nb = nx // bx
    u_bands = [16] * (yc // 16) if yc % 16 == 0 else [yc]
    planes = next(p for p in (2, 1) if zc % p == 0)
    wide = next(p for p in (8, 4, 2, 1) if zc % p == 0)
    length = -(-max(x_faces.shape[0], y_faces.shape[0], z_faces.shape[0]) // LANES) * LANES
    hbm = pl.BlockSpec(memory_space=pltpu.HBM)
    vmem = pl.BlockSpec(memory_space=pltpu.VMEM)
    there = functools.partial(pltpu.with_memory_space_constraint, memory_space=pltpu.HBM)

    def on_chip(*shape, dtype=f32):
        return pltpu.VMEM(shape, dtype)

    dma = pltpu.SemaphoreType.DMA
    base, sy, sz, zpass, ypass = pl.pallas_call(
        functools.partial(main_kernel, nr, nc, planes, wide, u_bands),
        in_specs=[hbm] * 5,
        out_specs=[vmem] * 5,
        out_shape=[
            on_chip(nt, zc, yc, LANES),
            on_chip(2, nt, zc, LANES),
            on_chip(2, nt, yc, LANES),
            on_chip(2, zc, LANES),
            on_chip(2, yc, LANES),
        ],
        scratch_shapes=[
            on_chip(3, 8, length),
            on_chip(nt, zc, yc + 16, LANES),
            on_chip(2, nt, zc, LANES),
            on_chip(2, nt, zc, LANES),
            on_chip(nt, yc, LANES),
            on_chip(2, nt, LANES),
            on_chip(2, yc, LANES),
            on_chip(4, zc, LANES),
            on_chip(8, nx),
            on_chip(nb, 3 * bx, bx, dtype=bf16),
            on_chip(2, nt, LANES),
            on_chip(2, nb, LANES),
            on_chip(yc, 3 * yc, dtype=bf16),
            on_chip(11, yc, LANES),
            on_chip(nt, zc, yc, LANES),
            on_chip(2, nr, LANES),
            on_chip(nt, yc, LANES),
            on_chip(2, nk, nt, 8, LANES),
            on_chip(nk, nt, 8, LANES),
            on_chip(2, nk, nt, 8, LANES),
            on_chip(nk, nt, 8, LANES),
            on_chip(8, LANES),
            on_chip(2, nt, zc, LANES),
            on_chip(2, nr, nt, zc, LANES),
            on_chip(2, nt, 2, LANES),
            on_chip(2, nr, nt, 2, LANES),
            on_chip(2, nt, yc, LANES),
            dma((3,)), dma((len(u_bands), nt)), dma((nk, nt)), dma((2,)), dma((2,)), dma((nk,)), dma((nk,)), dma((nk,)),
            dma((nk,)), dma((nk,)), dma((nk,)), dma((2, nr)), dma((2, nr)), dma((2, nr)), dma((2, nr)),
        ],
        compiler_params=pltpu.CompilerParams(
            collective_id=0, has_side_effects=True, vmem_limit_bytes=MAIN_VMEM
        ),
    )(there(x_faces[None]), there(y_faces[None]), there(z_faces[None]), there(u), there(reaction))

    last = next(p for p in (2, 1) if zc % p == 0)
    return pl.pallas_call(
        functools.partial(finish_kernel, last),
        in_specs=[vmem] * 5,
        out_specs=hbm,
        out_shape=jax.ShapeDtypeStruct((zc, yc, nx), f32),
        scratch_shapes=[on_chip(zc, yc, nx), dma((zc // last,))],
        compiler_params=pltpu.CompilerParams(vmem_limit_bytes=LAST_VMEM),
    )(base, sy, sz, zpass, ypass)


def solution(mesh):
    in_specs = (P("col", "row", None), P("col", "row", None), P(), P(), P(), P(), P(), P())
    out_specs = P("col", "row", None)
    return jax.shard_map(body, mesh=mesh, in_specs=in_specs, out_specs=out_specs, check_vma=False)
```

```python
import functools

import jax
import jax.numpy as jnp
from jax import lax
from jax.experimental import pallas as pl
from jax.experimental.pallas import tpu as pltpu
from jax.sharding import PartitionSpec as P

WEIGHT = 0.5
STEP = 1000.0
MESH = pl.DeviceIdType.MESH
LANES = 128
TOGETHER = 4
MAIN_VMEM = 32 * 1024 * 1024
LAST_VMEM = 12 * 1024 * 1024
FIRST_NS, HOP_NS, CHUNK_NS = 1100, 2100, 250
SECOND_NS, TABLE_NS, THIRD_NS = 330, 150, 1350


def shifted(a, by, fill):
    n = a.shape[1]
    lane = lax.broadcasted_iota(jnp.int32, a.shape, 1)
    if by > 0:
        return jnp.where(lane >= by, pltpu.roll(a, by, 1), fill)
    return jnp.where(lane < n + by, pltpu.roll(a, n + by, 1), fill)


def running_sum(a):
    by = 1
    while by < a.shape[1]:
        a = a + shifted(a, by, 0.0)
        by *= 2
    return a


def ladder(couple, sign):
    p00, p01, p10, p11 = 1.0 + couple, couple, jnp.ones_like(couple), couple
    by = 1
    while by < couple.shape[1]:
        q00, q01 = shifted(p00, sign * by, 1.0), shifted(p01, sign * by, 0.0)
        q10, q11 = shifted(p10, sign * by, 0.0), shifted(p11, sign * by, 1.0)
        n00, n01 = p00 * q00 + p01 * q10, p00 * q01 + p01 * q11
        n10, n11 = p10 * q00 + p11 * q10, p10 * q01 + p11 * q11
        scale = 1.0 / (n00 + n01 + n10 + n11)
        p00, p01, p10, p11 = n00 * scale, n01 * scale, n10 * scale, n11 * scale
        by *= 2
    return p00 / p10


def as_column(line, rows):
    n = line.shape[1]
    return jnp.transpose(jnp.broadcast_to(line, (n, n)))[:rows, :rows]


def block_of_inverse(diagonal, sums, n):
    i = lax.broadcasted_iota(jnp.int32, (n, n), 0)
    j = lax.broadcasted_iota(jnp.int32, (n, n), 1)
    near = jnp.where(i >= j, diagonal[:, :n], as_column(diagonal, n))
    return near * jnp.exp(-jnp.abs(as_column(sums, n) - sums[:, :n]))


def split(a):
    high = a.astype(jnp.bfloat16)
    return high, (a - high.astype(jnp.float32)).astype(jnp.bfloat16)


def dot(a, b):
    return jnp.dot(a, b, preferred_element_type=jnp.float32)


def lanes_of(column):
    return jnp.broadcast_to(column, (column.shape[0], LANES))


def x_solve(rows_of, xw, xpass, xthrough, nt):
    nb, bx = xw.shape[0], xw.shape[2]
    per = bx // LANES
    local = []
    for b in range(nb):
        high, low = split(jnp.concatenate([rows_of(b * per + i) for i in range(per)], axis=1))
        local.append(dot(jnp.concatenate([high, low, high], axis=1), xw[b]))
    left, right = [None], [None]
    for b in range(nb - 1):
        value = lanes_of(local[b][:, bx - 1:bx])
        if b:
            value = value + left[-1] * xthrough[0, b:b + 1]
        left.append(value)
        c = nb - 1 - b
        value = lanes_of(local[c][:, 0:1])
        if b:
            value = value + right[-1] * xthrough[1, c:c + 1]
        right.append(value)
    right.reverse()
    solved = []
    for t in range(nt):
        b, i = t // per, t % per
        value = local[b][:, i * LANES:(i + 1) * LANES]
        if b:
            value = value + xpass[0, t:t + 1] * left[b]
        if b < nb - 1:
            value = value + xpass[1, t:t + 1] * right[b]
        solved.append(value)
    return solved


def main_kernel(
    nr, nc, planes, wide, u_bands, xf_hbm, yf_hbm, zf_hbm, field_ref, rea_ref,
    base, sy_ref, sz_ref, zpass, ypass,
    faces, u, edges, yhalo, coef, xface, yface, ztab, xline, xw, xpass, xthrough, ym, ysolve, along, weights,
    vprev, zedge, zsend, zbuf, pbuf, through, ye, ybuf, esend, ebuf, fill,
    face_sem, u_sem, rea_sem, hsend, hrecv, zsend_sem, zrecv_sem, psend_sem, precv_sem,
    fsend_sem, frecv_sem, ysend_sem, yrecv_sem, esend_sem, erecv_sem,
):
    row, col = lax.axis_index("row"), lax.axis_index("col")
    nt, zc, yc, _ = base.shape
    nx = nt * LANES
    nk = yc // 8
    length = faces.shape[2]
    f32 = jnp.float32

    face_copies = [
        pltpu.make_async_copy(
            a, faces.at[i, pl.ds(0, 1), pl.ds(0, a.shape[1])], face_sem.at[i]
        )
        for i, a in enumerate((xf_hbm, yf_hbm, zf_hbm))
    ]
    for i, a in enumerate((xf_hbm, yf_hbm, zf_hbm)):
        if a.shape[1] < length:
            faces[i, 0:1, a.shape[1]:] = jnp.zeros((1, length - a.shape[1]), f32)
    for copy in face_copies:
        copy.start()
    bands = len(u_bands)
    first_row = [sum(u_bands[:i]) for i in range(bands)]

    def u_copy(i, t):
        return pltpu.make_async_copy(
            field_ref.at[:, pl.ds(first_row[i], u_bands[i]), pl.ds(t * LANES, LANES)],
            u.at[t, :, pl.ds(8 + first_row[i], u_bands[i])], u_sem.at[i, t],
        )

    def rea_copy(k, t):
        rows = pl.ds(k * 8 if isinstance(k, int) else pl.multiple_of(k * 8, 8), 8)
        return pltpu.make_async_copy(
            rea_ref.at[:, rows, pl.ds(t * LANES, LANES)], base.at[t, :, rows], rea_sem.at[k, t]
        )

    waiting = [(k + 1) % nk for k in range(nk)]
    for i in [0, bands - 1] + list(range(1, bands - 1)) if bands > 1 else [0]:
        for t in range(nt):
            u_copy(i, t).start()
        if i >= min(1, bands - 1) and i < bands - 1 or bands <= 2 and i == bands - 1:
            for k in waiting[:2]:
                for t in range(nt):
                    rea_copy(k, t).start()
            waiting = waiting[2:]
    for k in waiting:
        for t in range(nt):
            rea_copy(k, t).start()

    up_row, down_row = row < nr - 1, row > 0
    core, chip, chips = lax.rem(col, 2), col // 2, nc // 2
    mine, theirs = 1 - core, core
    far = jnp.where(core == 1, chip, chips - 1 - chip)
    chained, chains, fed = far > 0, far < chips - 1, far < chips - 1
    partner, following = col + 1 - 2 * core, col + 2 * (2 * core - 1)
    below, beyond = col >= 2, col < nc - 2
    barrier = pltpu.get_barrier_semaphore()
    for other in range(nr):
        @pl.when(other != row)
        def _():
            pl.semaphore_signal(barrier, inc=1, device_id=(other, col), device_id_type=MESH)

    pl.semaphore_signal(barrier, inc=1, device_id=(row, partner), device_id_type=MESH)

    @pl.when(below)
    def _():
        pl.semaphore_signal(barrier, inc=1, device_id=(row, col - 2), device_id_type=MESH)

    @pl.when(beyond)
    def _():
        pl.semaphore_signal(barrier, inc=1, device_id=(row, col + 2), device_id_type=MESH)

    vprev[...] = jnp.zeros_like(vprev)
    for side, there in ((0, down_row), (1, up_row)):
        source = chip > 0 if side == 0 else chip < chips - 1

        @pl.when(jnp.logical_not(source))
        def _():
            zbuf[side] = jnp.zeros(zbuf.shape[1:], f32)

        @pl.when(jnp.logical_not(there))
        def _():
            yhalo[side] = jnp.zeros(yhalo.shape[1:], f32)

    for copy in face_copies:
        copy.wait()

    lines = jnp.concatenate([faces[0, 0:1], faces[1, 0:1], faces[2, 0:1], jnp.zeros((5, length), f32)], axis=0)
    here = WEIGHT * STEP * lines
    above = shifted(here, -1, 0.0)
    e = ladder(here, 1)
    h = ladder(above, -1)
    pivot = above + e
    down = above / pivot
    inverse = 1.0 / pivot
    diag = 1.0 / (e + h - 1.0)
    ups = running_sum(jnp.log(jnp.maximum(here / (here + h), 1e-30)))
    downs = running_sum(jnp.log(jnp.maximum(down, 1e-30)))
    ups_before, downs_before = shifted(ups, 1, 0.0), shifted(downs, 1, 0.0)
    next_lines = shifted(lines, -1, 0.0)
    around = lines + next_lines

    xline[0:1] = diag[0:1, :nx]
    xline[1:2] = ups[0:1, :nx]
    xline[2:3] = ups_before[0:1, :nx]
    xline[3:4] = downs[0:1, :nx]
    xline[4:5] = downs_before[0:1, :nx]
    before = shifted(next_lines, 1, 0.0)
    for t in range(nt):
        cols = slice(t * LANES, (t + 1) * LANES)
        xface[0, t:t + 1] = before[0:1, cols]
        xface[1, t:t + 1] = next_lines[0:1, cols]

    def own(values, which, start):
        shift = lax.rem(length - start, length)
        return pltpu.roll(values, shift, 1)[which:which + 1]

    def passes(which, start, count):
        u0, d0 = own(ups_before, which, start)[:, 0:1], own(downs_before, which, start)
        u1, d1 = own(ups, which, start), own(downs, which, start)[:, count - 1:count]
        return u1, u0, d1, jnp.exp(jnp.minimum(u1 - u0, 0.0)), jnp.exp(jnp.minimum(d1 - d0, 0.0))

    def columns(given):
        filled = [a[:, :LANES] for a in given] + [jnp.zeros((LANES - len(given), LANES), f32)]
        return jnp.transpose(jnp.concatenate(filled, axis=0))

    z0 = col * zc
    zsums, _, _, onward, backward = passes(2, z0, zc)
    at = lax.broadcasted_iota(jnp.int32, (1, length), 1)
    zdiag = own(diag, 2, z0)
    over = jnp.where(at == zc - 1, zdiag, own(inverse, 2, z0))
    into = jnp.where(at == 0, 0.0, own(here, 2, z0) * over)
    low_end = zdiag[:, 0:1] * jnp.exp(jnp.minimum(zsums - zsums[:, 0:1], 0.0))
    scale = WEIGHT * STEP
    turned = columns([scale * over, into, scale * low_end, own(down, 2, z0), onward, backward])
    for i in range(4):
        ztab[i] = lanes_of(turned[:zc, i:i + 1])
    for i in range(2):
        zpass[i] = lanes_of(turned[:zc, 4 + i:5 + i])
    _, _, _, ponward, pbackward = passes(2, partner * zc, zc)
    here_on = jnp.where(core == 1, onward[:, zc - 1:zc], backward[:, 0:1])
    first_on = jnp.where(core == 1, ponward[:, zc - 1:zc], pbackward[:, 0:1])
    for i, value in enumerate((here_on, first_on, here_on * first_on)):
        through[i:i + 1] = lanes_of(value)

    y0 = row * yc
    sums, up_first, down_last, onward, backward = passes(1, y0, yc)
    ky, kyn, kya = own(lines, 1, y0), own(next_lines, 1, y0), own(around, 1, y0)
    seg = yc // 8
    place = lax.rem(at, seg)
    yups, yups_before = own(ups, 1, y0), own(ups_before, 1, y0)
    ydowns, ydowns_before = own(downs, 1, y0), own(downs_before, 1, y0)
    begins, ends = yups_before, ydowns
    for j in range(1, seg):
        begins = jnp.where(place == j, pltpu.roll(yups_before, j, 1), begins)
        ends = jnp.where(place == seg - 1 - j, pltpu.roll(ydowns, length - j, 1), ends)

    def decay(a):
        return jnp.exp(jnp.minimum(a, 0.0))

    seg_over = jnp.where(place == seg - 1, own(diag, 1, y0), own(inverse, 1, y0))
    seg_lines = [
        seg_over,
        jnp.where(place == 0, 0.0, own(here, 1, y0) * seg_over),
        own(down, 1, y0),
        jnp.where(at < seg, 0.0, decay(yups - begins)),
        jnp.where(at >= yc - seg, 0.0, decay(ends - ydowns_before)),
    ]
    for d in (1, 2, 4):
        value = decay(yups - pltpu.roll(yups, d * seg, 1))
        seg_lines.append(jnp.where(at < d * seg, 0.0, value))
    for d in (1, 2, 4):
        value = decay(pltpu.roll(ydowns_before, length - d * seg, 1) - ydowns_before)
        seg_lines.append(jnp.where(at >= yc - d * seg, 0.0, value))
    turned = columns([ky, kyn, 1.0 / scale - kya, onward, backward] + seg_lines)
    for i in range(len(seg_lines)):
        ysolve[i] = lanes_of(turned[:yc, 5 + i:6 + i])
    yface[0] = lanes_of(turned[:yc, 0:1])
    yface[1] = lanes_of(turned[:yc, 1:2])
    ypass[0] = lanes_of(turned[:yc, 3:4])
    ypass[1] = lanes_of(turned[:yc, 4:5])
    ycoef = lanes_of(turned[:yc, 2:3])
    for t in range(nt):
        coef[t] = ycoef - around[0:1, t * LANES:(t + 1) * LANES]
    block = block_of_inverse(own(diag, 1, y0)[:, :LANES], sums[:, :LANES], LANES)[:yc, :yc]
    high, low = split(block)
    ym[...] = jnp.concatenate([high, high, low], axis=1)
    for other in range(nr):
        last, first = (other + 1) * yc - 1, other * yc
        value = jnp.exp(jnp.minimum(up_first - ups[1:2, last:last + 1], 0.0))
        weights[0, other:other + 1] = lanes_of(value)
        value = jnp.exp(jnp.minimum(downs_before[1:2, first:first + 1] - down_last, 0.0))
        weights[1, other:other + 1] = lanes_of(value)

    for i in sorted({0, bands - 1}):
        for t in range(nt):
            u_copy(i, t).wait()

    def take_edges(z, _):
        for t in range(nt):
            edges[0, t, pl.ds(z, 1)] = u[t, z, 8 + yc - 1:8 + yc]
            edges[1, t, pl.ds(z, 1)] = u[t, z, 8:9]
        return 0

    lax.fori_loop(0, zc, take_edges, 0, unroll=4 if zc % 4 == 0 else 1)
    pl.semaphore_wait(barrier, nr + below.astype(jnp.int32) + beyond.astype(jnp.int32))

    def halo(side):
        return pltpu.make_async_remote_copy(
            src_ref=edges.at[side], dst_ref=yhalo.at[side],
            send_sem=hsend.at[side], recv_sem=hrecv.at[side],
            device_id=(row + 1 - 2 * side, col), device_id_type=MESH,
        )

    for side, to in ((0, up_row), (1, down_row)):
        @pl.when(to)
        def _():
            halo(side).start()

    def pair_copy(k):
        return pltpu.make_async_remote_copy(
            src_ref=zedge.at[theirs, k], dst_ref=pbuf.at[k],
            send_sem=psend_sem.at[k], recv_sem=precv_sem.at[k],
            device_id=(row, partner), device_id_type=MESH,
        )

    def chain_copy(k):
        return pltpu.make_async_remote_copy(
            src_ref=zsend.at[k], dst_ref=zbuf.at[mine, k],
            send_sem=zsend_sem.at[k], recv_sem=zrecv_sem.at[k],
            device_id=(row, following), device_id_type=MESH,
        )

    def forward_copy(k):
        return pltpu.make_async_remote_copy(
            src_ref=zbuf.at[mine, k], dst_ref=zbuf.at[mine, k],
            send_sem=fsend_sem.at[k], recv_sem=frecv_sem.at[k],
            device_id=(row, partner), device_id_type=MESH,
        )

    def relay(k):
        pair_copy(k).wait_recv()

        @pl.when(chained)
        def _():
            chain_copy(k).wait_recv()
            forward_copy(k).start()

        @pl.when(chains)
        def _():
            own_on, both_on = through[0:1], through[2:3]
            for t in range(nt):
                value = zedge[mine, k, t] + own_on * pbuf[k, t]
                zsend[k, t] = value + both_on * zbuf[mine, k, t]
            chain_copy(k).start()

    def chunk_at(j):
        return lax.rem(j + 1, nk)

    lag = 3 * far

    lane = lax.broadcasted_iota(jnp.int32, (8, LANES), 1)
    group = min(nt, 8)

    long = next(n for n in (16, 8, 4, 2, 1) if zc % n == 0)

    def first_pass(i, _):
        k = lax.rem(i + 1, nk)
        y = pl.multiple_of(k * 8, 8)
        rows = pl.ds(y, 8)
        for t in range(nt):
            rea_copy(k, t).wait()

        for b in range(1, bands - 1):
            @pl.when(i == max(first_row[b] // 8 - 2, 0))
            def _():
                for t in range(nt):
                    u_copy(b, t).wait()

        @pl.when(i == nk - 2)
        def _():
            for side, there in ((0, down_row), (1, up_row)):
                @pl.when(there)
                def _():
                    halo(side).wait_recv()

            def put(z, _):
                for t in range(nt):
                    u[t, z, 7:8] = yhalo[0, t, pl.ds(z, 1)]
                    u[t, z, 8 + yc:9 + yc] = yhalo[1, t, pl.ds(z, 1)]
                return 0

            lax.fori_loop(0, zc, put, 0, unroll=4 if zc % 4 == 0 else 1)

        for g in range(nt // group):
            tiles = [g * group + i for i in range(group)]

            def one(z, carried):
                tops, lows = carried
                over, into, low_end = ztab[0, pl.ds(z, 1)], ztab[1, pl.ds(z, 1)], ztab[2, pl.ds(z, 1)]
                kyd, kyu = yface[0, rows], yface[1, rows]
                middle = [u[t % nt, z, pl.ds(y + 8, 8)] for t in range(tiles[0] - 1, tiles[-1] + 2)] \
                    if group < nt else [u[t, z, pl.ds(y + 8, 8)] for t in tiles]
                from_low = [pltpu.roll(a, 1, 1) for a in middle]
                from_high = [pltpu.roll(a, LANES - 1, 1) for a in middle]
                n, shift = len(middle), 1 if group < nt else 0
                new_tops, new_lows = [], []
                for j, t in enumerate(tiles):
                    m = j + shift
                    c = middle[m]
                    left = jnp.where(lane == 0, from_low[(m - 1) % n], from_low[m])
                    right = jnp.where(lane == LANES - 1, from_high[(m + 1) % n], from_high[m])
                    q = base[t, z, rows] * (1.0 - c * c) + coef[t, rows]
                    value = q * c + (xface[1, t:t + 1] * right + xface[0, t:t + 1] * left)
                    value = value + (kyu * u[t, z, pl.ds(y + 9, 8)] + kyd * u[t, z, pl.ds(y + 7, 8)])
                    top = over * value + into * tops[j]
                    base[t, z, rows] = top
                    new_tops.append(top)
                    new_lows.append(lows[j] + low_end * value)
                return new_tops, new_lows

            zero = [jnp.zeros((8, LANES), f32) for _ in tiles]
            tops, lows = lax.fori_loop(0, zc, one, (zero, zero), unroll=long)
            for j, t in enumerate(tiles):
                zedge[0, k, t] = tops[j]
                zedge[1, k, t] = lows[j]

        pair_copy(k).start()
        turn = i - 1 - lag

        @pl.when(turn >= 0)
        def _():
            relay(chunk_at(turn))

        return 0

    lax.fori_loop(0, nk, first_pass, 0)

    due = FIRST_NS + HOP_NS * far
    begun = jnp.maximum(nk - 1 - lag, 0)

    def count(now):
        ahead = (jnp.maximum(now - due + nk * CHUNK_NS, 0)) // CHUNK_NS
        return jnp.clip(ahead, begun, nk)

    def relays(since, now):
        def one(j, _):
            relay(chunk_at(j))
            return 0

        lax.fori_loop(count(since), count(now), one, 0)

    per = 256 // LANES
    steps = zc // planes

    def y_solve(tiles):
        high, low = split(jnp.concatenate(tiles, axis=1))
        return dot(ym[...], jnp.concatenate([high, low, high], axis=0))

    def segments(j):
        return pl.ds(j, 8, stride=seg)

    def y_lines(lines):
        w = [[] for _ in lines]
        for j in range(seg):
            over, into = ysolve[0, segments(j)], ysolve[1, segments(j)]
            for i, (_, _, ready) in enumerate(lines):
                value = over * ready[j]
                w[i].append(value + into * w[i][-1] if j else value)
        v = [[a[-1]] for a in w]
        for j in range(seg - 2, -1, -1):
            onto = ysolve[2, segments(j)]
            for i in range(len(lines)):
                v[i].append(w[i][j] + onto * v[i][-1])
        rising, falling = [a[0] for a in v], [a[-1] for a in v]
        for k, d in enumerate((1, 2, 4)):
            up, back = ysolve[5 + k, segments(seg - 1)], ysolve[8 + k, segments(0)]
            rising = [a + up * pltpu.roll(a, d, 0) for a in rising]
            falling = [a + back * pltpu.roll(a, 8 - d, 0) for a in falling]
        rising, falling = [pltpu.roll(a, 1, 0) for a in rising], [pltpu.roll(a, 7, 0) for a in falling]
        for j in range(seg):
            up, back = ysolve[3, segments(j)], ysolve[4, segments(j)]
            for i, (t, z, _) in enumerate(lines):
                value = v[i][seg - 1 - j] + (up * rising[i] + back * falling[i])
                along[t, z, segments(j)] = value
                if j == 0:
                    ye[0, t, pl.ds(z, 1)] = value[0:1]
                if j == seg - 1:
                    ye[1, t, pl.ds(z, 1)] = value[7:8]

    def second_pass(slot, _):
        for p in range(planes):
            z = zc - 1 - (slot * planes + p)
            onto = ztab[3, pl.ds(z, 1)]
            solved = []
            for b in range(nt // per - 1):
                ready = []
                for t in range(b * per, (b + 1) * per):
                    v = base[t, z] + onto * vprev[t]
                    vprev[t] = v
                    ready.append(v - u[t, z, 8:8 + yc])
                solved.append(y_solve(ready))
            for g in range(1):
                lines = []
                for t in range(nt - per, nt):
                    ready = []
                    for j in range(seg):
                        v = base[t, z, segments(j)] + onto * vprev[t, j * 8:(j + 1) * 8]
                        vprev[t, j * 8:(j + 1) * 8] = v
                        ready.append(v - u[t, z, pl.ds(8 + j, 8, stride=seg)])
                    lines.append((t, z, ready))
                y_lines(lines)
            for b, both in enumerate(solved):
                for i in range(per):
                    t = b * per + i
                    part = both[:, i * LANES:(i + 1) * LANES]
                    along[t, z] = part
                    ye[0, t, pl.ds(z, 1)] = part[0:1]
                    ye[1, t, pl.ds(z, 1)] = part[yc - 1:yc]
        relays(SECOND_NS * slot, SECOND_NS * (slot + 1))
        return 0

    lax.fori_loop(0, steps, second_pass, 0)
    now = SECOND_NS * steps

    def y_copy(side, other, slot):
        return pltpu.make_async_remote_copy(
            src_ref=ye.at[1 - side], dst_ref=ybuf.at[side, slot],
            send_sem=ysend_sem.at[side, other], recv_sem=yrecv_sem.at[side, slot],
            device_id=(other, col), device_id_type=MESH,
        )

    for other in range(nr):
        @pl.when(other > row)
        def _():
            y_copy(0, other, row).start()

        @pl.when(other < row)
        def _():
            y_copy(1, other, row).start()

    nb, bx = xw.shape[0], xw.shape[2]
    for b in range(nb):
        cols = slice(b * bx, (b + 1) * bx)
        first, last = b * bx, (b + 1) * bx - 1
        high, low = split(block_of_inverse(xline[0:1, cols], xline[1:2, cols], bx) * (1.0 / WEIGHT))
        xw[b, 0:bx] = high
        xw[b, bx:2 * bx] = high
        xw[b, 2 * bx:3 * bx] = low
        ahead = jnp.exp(xline[1:2, cols] - xline[2:3, first:first + 1])
        back = jnp.exp(xline[3:4, last:last + 1] - xline[4:5, cols])
        for i in range(bx // LANES):
            t = b * (bx // LANES) + i
            xpass[0, t:t + 1] = ahead[:, i * LANES:(i + 1) * LANES]
            xpass[1, t:t + 1] = back[:, i * LANES:(i + 1) * LANES]
        xthrough[0, b:b + 1] = lanes_of(ahead[:, bx - 1:bx])
        xthrough[1, b:b + 1] = lanes_of(back[:, 0:1])
        relays(now, now + TABLE_NS)
        now += TABLE_NS

    def third(slot):
        zs = [slot * wide + p for p in range(wide)]
        solved = x_solve(
            lambda t: jnp.concatenate([along[t, z] for z in zs], axis=0), xw, xpass, xthrough, nt
        )
        for t in range(nt):
            for p, z in enumerate(zs):
                base[t, z] = u[t, z, 8:8 + yc] + solved[t][p * yc:(p + 1) * yc]

    def third_pass(slot, _):
        third(slot)
        relays(now + THIRD_NS * slot, now + THIRD_NS * (slot + 1))
        return 0

    early = (zc // wide + 1) // 2
    lax.fori_loop(0, early, third_pass, 0)
    relays(now + THIRD_NS * early, 1 << 30)

    @pl.when(fed)
    def _():
        for k in range(nk):
            forward_copy(k).wait_recv()

    for which in range(2):
        k = theirs if which else mine
        for b in range(nt // per):
            tiles = []
            for t in range(b * per, (b + 1) * per):
                pieces = [zbuf[k, j, t] for j in range(nk)]
                if not which:
                    pieces = [pbuf[j, t] + through[1:2] * pieces[j] for j in range(nk)]
                tiles.append(jnp.concatenate(pieces, axis=0))
            solved = y_solve(tiles)
            for i in range(per):
                t = b * per + i
                part = solved[:, i * LANES:(i + 1) * LANES]
                fill[k, t] = part
                esend[0, t, pl.ds(k, 1)] = part[yc - 1:yc]
                esend[1, t, pl.ds(k, 1)] = part[0:1]

    def e_copy(side, other, slot):
        return pltpu.make_async_remote_copy(
            src_ref=esend.at[side], dst_ref=ebuf.at[side, slot],
            send_sem=esend_sem.at[side, other], recv_sem=erecv_sem.at[side, slot],
            device_id=(other, col), device_id_type=MESH,
        )

    for other in range(nr):
        @pl.when(other > row)
        def _():
            e_copy(0, other, row).start()

        @pl.when(other < row)
        def _():
            e_copy(1, other, row).start()

    def last_pass(slot, _):
        third(slot)
        return 0

    lax.fori_loop(early, zc // wide, last_pass, 0)

    sy_ref[...] = jnp.zeros_like(sy_ref)
    for other in range(nr):
        for side, there in ((0, other < row), (1, other > row)):
            @pl.when(there)
            def _():
                y_copy(side, other, other).wait_recv()
                for t in range(nt):
                    sy_ref[side, t] += weights[side, other:other + 1] * ybuf[side, other, t]

    for other in range(nr):
        for side, there in ((0, other < row), (1, other > row)):
            @pl.when(there)
            def _():
                e_copy(side, other, other).wait_recv()
                coefficients = weights[side, other:other + 1] * ypass[side]
                for t in range(nt):
                    for k in range(2):
                        fill[k, t] += coefficients * ebuf[side, other, t, k:k + 1]

    solved = x_solve(
        lambda t: jnp.concatenate([fill[0, t], fill[1, t], sy_ref[0, t], sy_ref[1, t]], axis=0),
        xw, xpass, xthrough, nt,
    )
    for t in range(nt):
        sz_ref[0, t] = solved[t][:yc]
        sz_ref[1, t] = solved[t][yc:2 * yc]
        sy_ref[0, t] = solved[t][2 * yc:2 * yc + zc]
        sy_ref[1, t] = solved[t][2 * yc + zc:]

    for side, to in ((0, up_row), (1, down_row)):
        @pl.when(to)
        def _():
            halo(side).wait_send()

    for k in range(nk):
        pair_copy(k).wait_send()

        @pl.when(chained)
        def _():
            forward_copy(k).wait_send()

        @pl.when(chains)
        def _():
            chain_copy(k).wait_send()

    for other in range(nr):
        for side, there in ((0, other > row), (1, other < row)):
            @pl.when(there)
            def _():
                y_copy(side, other, row).wait_send()
                e_copy(side, other, row).wait_send()


def finish_kernel(planes, base, sy_ref, sz_ref, zpass, ypass, out_ref, staged, sem):
    nt, zc = base.shape[0], base.shape[1]

    def out_copy(i):
        part = pl.ds(i * planes, planes)
        return pltpu.make_async_copy(staged.at[part], out_ref.at[part], sem.at[i])

    def one(i, _):
        for p in range(planes):
            z = i * planes + p
            zb, za = zpass[0, pl.ds(z, 1)], zpass[1, pl.ds(z, 1)]
            for t in range(nt):
                value = base[t, z] + (
                    ypass[0] * sy_ref[0, t, pl.ds(z, 1)] + ypass[1] * sy_ref[1, t, pl.ds(z, 1)]
                )
                value = value + (zb * sz_ref[0, t] + za * sz_ref[1, t])
                staged[z, :, t * LANES:(t + 1) * LANES] = value
        out_copy(i).start()
        return 0

    lax.fori_loop(0, zc // planes, one, 0)

    def end(i, _):
        out_copy(i).wait()
        return 0

    lax.fori_loop(0, zc // planes, end, 0)


def body(u, reaction, x_faces, y_faces, z_faces, x_inverse, y_inverse, z_inverse):
    zc, yc, nx = u.shape
    nr, nc = lax.axis_size("row"), lax.axis_size("col")
    f32, bf16 = jnp.float32, jnp.bfloat16
    nt, nk = nx // LANES, yc // 8
    bx = 256
    nb = nx // bx
    u_bands = [16] * (yc // 16) if yc % 16 == 0 else [yc]
    planes = next(p for p in (2, 1) if zc % p == 0)
    wide = next(p for p in (8, 4, 2, 1) if zc % p == 0)
    length = -(-max(x_faces.shape[0], y_faces.shape[0], z_faces.shape[0]) // LANES) * LANES
    hbm = pl.BlockSpec(memory_space=pltpu.HBM)
    vmem = pl.BlockSpec(memory_space=pltpu.VMEM)
    there = functools.partial(pltpu.with_memory_space_constraint, memory_space=pltpu.HBM)

    def on_chip(*shape, dtype=f32):
        return pltpu.VMEM(shape, dtype)

    dma = pltpu.SemaphoreType.DMA
    base, sy, sz, zpass, ypass = pl.pallas_call(
        functools.partial(main_kernel, nr, nc, planes, wide, u_bands),
        in_specs=[hbm] * 5,
        out_specs=[vmem] * 5,
        out_shape=[
            on_chip(nt, zc, yc, LANES),
            on_chip(2, nt, zc, LANES),
            on_chip(2, nt, yc, LANES),
            on_chip(2, zc, LANES),
            on_chip(2, yc, LANES),
        ],
        scratch_shapes=[
            on_chip(3, 8, length),
            on_chip(nt, zc, yc + 16, LANES),
            on_chip(2, nt, zc, LANES),
            on_chip(2, nt, zc, LANES),
            on_chip(nt, yc, LANES),
            on_chip(2, nt, LANES),
            on_chip(2, yc, LANES),
            on_chip(4, zc, LANES),
            on_chip(8, nx),
            on_chip(nb, 3 * bx, bx, dtype=bf16),
            on_chip(2, nt, LANES),
            on_chip(2, nb, LANES),
            on_chip(yc, 3 * yc, dtype=bf16),
            on_chip(11, yc, LANES),
            on_chip(nt, zc, yc, LANES),
            on_chip(2, nr, LANES),
            on_chip(nt, yc, LANES),
            on_chip(2, nk, nt, 8, LANES),
            on_chip(nk, nt, 8, LANES),
            on_chip(2, nk, nt, 8, LANES),
            on_chip(nk, nt, 8, LANES),
            on_chip(8, LANES),
            on_chip(2, nt, zc, LANES),
            on_chip(2, nr, nt, zc, LANES),
            on_chip(2, nt, 2, LANES),
            on_chip(2, nr, nt, 2, LANES),
            on_chip(2, nt, yc, LANES),
            dma((3,)), dma((len(u_bands), nt)), dma((nk, nt)), dma((2,)), dma((2,)), dma((nk,)), dma((nk,)), dma((nk,)),
            dma((nk,)), dma((nk,)), dma((nk,)), dma((2, nr)), dma((2, nr)), dma((2, nr)), dma((2, nr)),
        ],
        compiler_params=pltpu.CompilerParams(
            collective_id=0, has_side_effects=True, vmem_limit_bytes=MAIN_VMEM
        ),
    )(there(x_faces[None]), there(y_faces[None]), there(z_faces[None]), there(u), there(reaction))

    last = next(p for p in (2, 1) if zc % p == 0)
    return pl.pallas_call(
        functools.partial(finish_kernel, last),
        in_specs=[vmem] * 5,
        out_specs=hbm,
        out_shape=jax.ShapeDtypeStruct((zc, yc, nx), f32),
        scratch_shapes=[on_chip(zc, yc, nx), dma((zc // last,))],
        compiler_params=pltpu.CompilerParams(vmem_limit_bytes=LAST_VMEM),
    )(base, sy, sz, zpass, ypass)


def solution(mesh):
    in_specs = (P("col", "row", None), P("col", "row", None), P(), P(), P(), P(), P(), P())
    out_specs = P("col", "row", None)
    return jax.shard_map(body, mesh=mesh, in_specs=in_specs, out_specs=out_specs, check_vma=False)
```
